32 devices in a mesh: grp: 4 (over y, core), col: 8 (over z, x).
Axes of the slice: x: 2, y: 2, z: 4, core: 2. Of those that a mesh axis runs over, the one named last changes fastest.
Arguments:
- descriptors: float32 [4096, 2000], P(('grp', 'col')), may hold values from 0 to 1
Outputs:
- kernel: float32 [4096, 4, 1024], P('grp', None, 'col')
The draws below stay inside these ranges and needn't reach their ends.
All inputs are finite; a program needn't handle non-finite values.
Results may differ from the reference program's by a relative error of at most 0.00056.
Values may be sent and summed in bfloat16 or wider, within the bound.
No kernel may reach another device: no remote copies, remote signals or barrier semaphores. Data moves between devices by JAX's collectives and lax.ppermute only.
A program may use at most 128 MiB of HBM per device.

```python
import jax
import jax.numpy as jnp
from jax import lax

FEAT = 2000
BLOCK = 128
POINTS = 4096
N_GRP = 4
N_COL = 8


def steps_of(rng, shape, shards, least, top_value):
    factor_of, own = 1.0, jax.random.fold_in(rng, 6)
    for axis_at, parts in shards:
        steps = jnp.exp(jax.random.uniform(jax.random.fold_in(own, axis_at), (parts,), jnp.float32, least / len(shards), top_value / len(shards)))
        factor_of = factor_of * jnp.repeat(steps, shape[axis_at] // parts).reshape([-1 if axis == axis_at else 1 for axis in range(len(shape))])
    return factor_of


def setup_inputs(seed: int = 0) -> dict:
    splits = jax.random.split(jax.random.key(seed), 2)
    return {
        "descriptors": jnp.clip(1.0 * jax.random.uniform(splits[0], (POINTS, FEAT), jnp.float32) ** steps_of(splits[0], (POINTS, FEAT), ((0, 32),), -0.2, 0.2), 0.0, 1.0),
    }


def reference(descriptors):
    squares = lax.optimization_barrier(jnp.sum(descriptors * descriptors, axis=1, keepdims=True))
    unit = (descriptors * jax.lax.rsqrt(squares + 1e-06)).astype(jnp.bfloat16)
    intersection = jnp.dot(unit, unit.T, preferred_element_type=jnp.float32)
    second = intersection * intersection
    kernel = second * second
    return kernel.reshape(POINTS, N_GRP, N_COL * BLOCK)
```

```python
import jax
import jax.numpy as jnp
from jax import lax
from jax.sharding import PartitionSpec as P

AXES = ("grp", "col")
LINE = 4
SCALE = 32768.0


def fourth(left, right):
    intersection = lax.dot_general(
        left, right, (((0,), (0,)), ((), ())), preferred_element_type=jnp.float32
    )
    second = intersection * intersection
    return second * second


def shards(descriptors):
    ngroups = lax.axis_size("grp")
    ncolumns = lax.axis_size("col")
    block = descriptors.shape[0]
    inner = ncolumns // LINE
    grp = lax.axis_index("grp")
    col = lax.axis_index("col")
    z, x = col // inner, col % inner
    middle = jnp.logical_or(z == 1, z == 2)

    def send(array, move):
        pairs = []
        for g in range(ngroups):
            for c in range(ncolumns):
                target = move(g, c // inner, c % inner)
                if target is not None:
                    tg, tz, tx = target
                    pairs.append((g * ncolumns + c, (tg * LINE + tz) * inner + tx))
        return lax.ppermute(array, AXES, pairs)

    def mid(zz):
        return zz in (1, 2)

    def shift(k):
        return lambda g, zz, xx: (g, zz, (xx - k) % inner)

    def only(test, move):
        return lambda g, zz, xx: move(g, zz, xx) if test(zz) else None

    def columns_of(unit, test):
        parts = [(unit, 0)]
        for j in range(2, ngroups, 2):
            parts.append((send(unit, only(test, lambda g, zz, xx: ((g - j) % ngroups, zz, xx))), j))
        full = jnp.zeros((ngroups,) + unit.shape, unit.dtype)
        for part, j in parts:
            other = send(part, only(test, lambda g, zz, xx: (g ^ 1, zz, xx)))
            full = lax.dynamic_update_index_in_dim(full, part, (grp + j) % ngroups, 0)
            full = lax.dynamic_update_index_in_dim(full, other, ((grp ^ 1) + j) % ngroups, 0)
        return full

    data = descriptors.T
    squares = jnp.sum(data * data, axis=0, keepdims=True)
    unit = (data * lax.rsqrt(squares + 1e-06)).astype(jnp.bfloat16)

    every = lambda zz: True
    end = lambda zz: not mid(zz)
    offsets = range(1, inner)
    pair = send(unit, lambda g, zz, xx: (g, zz ^ 1, xx))
    centre = send(unit, only(mid, lambda g, zz, xx: (g, zz ^ 3, xx)))
    across = [send(unit, shift(k)) for k in offsets]
    columns = columns_of(unit, every)
    relay = send(pair, lambda g, zz, xx: (g, zz ^ 3, xx) if mid(zz) else shift(1)(g, zz, xx))
    pair_across = [
        send(across[k - 1], only(end, lambda g, zz, xx: (g, zz ^ 1, xx))) for k in offsets
    ]
    end_across = [relay] + [send(pair, only(end, shift(k))) for k in range(2, inner)]
    centre_across = [send(centre, only(mid, shift(k))) for k in offsets]
    end_columns = columns_of(pair, mid)
    half = unit.shape[1] // 2
    far_across = []
    for k in offsets:
        first = send(pair_across[k - 1][:, :half], only(mid, lambda g, zz, xx: (g, zz ^ 3, xx)))
        second = send(relay[:, half:], only(mid, shift(k)))
        far_across.append(jnp.concatenate([first, second], axis=1))

    def panel(blocks, cols):
        out = fourth(jnp.concatenate(blocks, axis=1), cols)
        return out

    def product(rows, cols):
        intersection = lax.dot_general(
            rows, cols, (((0,), (1,)), ((), ())), preferred_element_type=jnp.float32
        )
        second = intersection * intersection
        return second * second

    far = [(centre, 3, 2, 0)] + [(b, 3, 2, k) for k, b in zip(offsets, centre_across)]
    far2 = [(relay, 2, 3, 0)] + [(b, 2, 3, k) for k, b in zip(offsets, far_across)]
    near = [(unit, 0, 0, 0)] + [(b, 0, 0, k) for k, b in zip(offsets, across)]
    near2 = [(pair, 1, 1, 0)]
    near2 += [(jnp.where(middle, a, b), 1, 1, k) for k, a, b in zip(offsets, pair_across, end_across)]

    out = jnp.zeros((ncolumns, block, ngroups, block), jnp.float32)

    def put(out, value, dz, k):
        at = (z ^ dz) * inner + (x + k) % inner
        return lax.dynamic_update_index_in_dim(out, value, at, 0)

    for b, dz, _, k in near + near2:
        out = put(out, product(b, columns), dz, k)
    to_end = only(mid, lambda g, zz, xx: (g, zz ^ 1, xx))
    for b, mz, ez, k in far + far2:
        own = product(b, columns)
        theirs = send((product(b, end_columns) * SCALE).astype(jnp.float16), to_end)
        value = jnp.where(middle, own, theirs.astype(jnp.float32) * (1.0 / SCALE))
        out = put(out, value, jnp.where(middle, mz, ez), k)
    return out.reshape(ncolumns * block, ngroups, block)


def plain(descriptors):
    squares = jnp.sum(descriptors * descriptors, axis=1, keepdims=True)
    unit = (descriptors * lax.rsqrt(squares + 1e-06)).astype(jnp.bfloat16)
    columns = lax.all_gather(unit, "grp", axis=0, tiled=True)
    rows = lax.all_gather(unit, "col", axis=0, tiled=True)
    return fourth(rows.T, columns.T).reshape(rows.shape[0], -1, unit.shape[0])


def solution(mesh):
    fits = mesh.shape["col"] % LINE == 0 and mesh.shape["grp"] % 2 == 0
    return jax.shard_map(
        shards if fits else plain,
        mesh=mesh,
        in_specs=(P(AXES, None),),
        out_specs=P("grp", None, "col"),
        check_vma=False,
    )
```

```python
import jax
import jax.numpy as jnp
from jax import lax
from jax.sharding import PartitionSpec as P

AXES = ("grp", "col")
LINE = 4
SCALE = 32768.0


def shards(descriptors):
    ngroups = lax.axis_size("grp")
    ncolumns = lax.axis_size("col")
    block = descriptors.shape[0]
    inner = ncolumns // LINE
    grp = lax.axis_index("grp")
    col = lax.axis_index("col")
    z, x = col // inner, col % inner
    middle = jnp.logical_or(z == 1, z == 2)

    def send(array, move):
        pairs = []
        for g in range(ngroups):
            for c in range(ncolumns):
                tg, tz, tx = move(g, c // inner, c % inner)
                pairs.append((g * ncolumns + c, (tg * LINE + tz) * inner + tx))
        return lax.ppermute(array, AXES, pairs)

    def mid(zz):
        return zz in (1, 2)

    def pairwise(g, zz, xx):
        return g, zz ^ 1, xx

    def centre_swap(g, zz, xx):
        return (g, zz ^ 3, xx) if mid(zz) else (g ^ 1, zz, xx)

    def core_swap(g, zz, xx):
        return g ^ 1, zz, xx

    def shift(k):
        return lambda g, zz, xx: (g, zz, (xx - k) % inner)

    def columns_of(unit):
        parts = [(unit, 0)]
        for j in range(2, ngroups, 2):
            parts.append((send(unit, lambda g, zz, xx: ((g - j) % ngroups, zz, xx)), j))
        full = jnp.zeros((ngroups,) + unit.shape, unit.dtype)
        for part, j in parts:
            other = send(part, core_swap)
            full = lax.dynamic_update_index_in_dim(full, part, (grp + j) % ngroups, 0)
            full = lax.dynamic_update_index_in_dim(full, other, ((grp ^ 1) + j) % ngroups, 0)
        return full

    data = descriptors.T
    squares = jnp.sum(data * data, axis=0, keepdims=True)
    unit = (data * lax.rsqrt(squares + 1e-06)).astype(jnp.bfloat16)

    offsets = range(1, inner)
    pair = send(unit, pairwise)
    centre = send(unit, centre_swap)
    across = [send(unit, shift(k)) for k in offsets]
    columns = columns_of(unit)
    relay = send(pair, centre_swap)
    pair_across = [send(a, pairwise) for a in across]
    centre_across = [send(centre, shift(k)) for k in offsets]
    end_columns = columns_of(pair)
    cut = unit.shape[0] // 32 * 16
    far_across = []
    for k in offsets:
        first = send(pair_across[k - 1][:cut], centre_swap)
        second = send(relay[cut:], shift(k))
        far_across.append(jnp.concatenate([first, second], axis=0))

    def product(rows, cols):
        intersection = lax.dot_general(
            rows, cols, (((0,), (1,)), ((), ())), preferred_element_type=jnp.float32
        )
        second = intersection * intersection
        return second * second

    out = jnp.zeros((ncolumns, block, ngroups, block), jnp.float32)

    def put(out, value, dz, k):
        at = (z ^ dz) * inner + (x + k) % inner
        return lax.dynamic_update_index_in_dim(out, value, at, 0)

    near = [(unit, 0, 0), (pair, 1, 0)]
    near += [(b, 0, k) for k, b in zip(offsets, across)]
    near += [(b, 1, k) for k, b in zip(offsets, pair_across)]
    for b, dz, k in near:
        out = put(out, product(b, columns), dz, k)
    far = [(centre, 3, 0), (relay, 2, 0)]
    far += [(b, 3, k) for k, b in zip(offsets, centre_across)]
    far += [(b, 2, k) for k, b in zip(offsets, far_across)]
    for b, dz, k in far:
        own = lax.optimization_barrier(product(b, columns))
        theirs = send((product(b, end_columns) * SCALE).astype(jnp.float16), pairwise)
        value = jnp.where(middle, own, theirs.astype(jnp.float32) * (1.0 / SCALE))
        out = put(out, value, jnp.where(middle, dz, dz ^ 1), k)
    return out.reshape(ncolumns * block, ngroups, block)


def plain(descriptors):
    squares = jnp.sum(descriptors * descriptors, axis=1, keepdims=True)
    unit = (descriptors * lax.rsqrt(squares + 1e-06)).astype(jnp.bfloat16)
    columns = lax.all_gather(unit, "grp", axis=0, tiled=True)
    rows = lax.all_gather(unit, "col", axis=0, tiled=True)
    intersection = jnp.dot(rows, columns.T, preferred_element_type=jnp.float32)
    second = intersection * intersection
    return (second * second).reshape(rows.shape[0], -1, unit.shape[0])


def solution(mesh):
    fits = mesh.shape["col"] % LINE == 0 and mesh.shape["grp"] % 2 == 0
    return jax.shard_map(
        shards if fits else plain,
        mesh=mesh,
        in_specs=(P(AXES, None),),
        out_specs=P("grp", None, "col"),
        check_vma=False,
    )
```

```python
import jax
import jax.numpy as jnp
from jax import lax
from jax.sharding import PartitionSpec as P


AXES = ("grp", "col")
LINE = 4
SCALE = 32768.0


def shards(descriptors):
    return exchange(descriptors)


def exchange(descriptors):
    ngroups = lax.axis_size("grp")
    ncolumns = lax.axis_size("col")
    block = descriptors.shape[0]
    inner = ncolumns // LINE
    offsets = range(1, inner)
    grp = lax.axis_index("grp")
    col = lax.axis_index("col")
    z, x = col // inner, col % inner
    middle = jnp.logical_or(z == 1, z == 2)

    def send(array, move):
        pairs = []
        for g in range(ngroups):
            for c in range(ncolumns):
                tg, tz, tx = move(g, c // inner, c % inner)
                pairs.append((g * ncolumns + c, (tg * LINE + tz) * inner + tx))
        return lax.ppermute(array, AXES, pairs)

    def line_swap(g, zz, xx):
        return g, zz ^ 1, xx

    def centre_swap(g, zz, xx):
        return (g, zz ^ 3, xx) if zz in (1, 2) else (g ^ 1, zz, xx)

    def core_swap(g, zz, xx):
        return g ^ 1, zz, xx

    def shift(k):
        return lambda g, zz, xx: (g, zz, (xx - k) % inner)

    def other(j):
        return lambda g, zz, xx: ((g - j) % ngroups, zz, xx)

    data = descriptors.T
    squares = jnp.sum(data * data, axis=0, keepdims=True)
    unit = (data * lax.rsqrt(squares + 1e-06)).astype(jnp.bfloat16)
    cut = unit.shape[0] // 32 * 16
    unit = [unit[:cut], unit[cut:]]
    others = range(2, ngroups, 2)
    pair, centre, relay = [None, None], [None, None], [None, None]
    across, pair_across, centre_across = ([[None, None] for _ in offsets] for _ in range(3))
    own = {(0, h): unit[h] for h in (0, 1)}
    end = {}

    for h in (0, 1):
        pair[h] = send(unit[h], line_swap)
        for k in offsets:
            across[k - 1][1 - h] = send(unit[1 - h], shift(k))
        centre[h] = send(unit[h], centre_swap)
        if h == 0:
            for j in others:
                own[j, 0] = send(unit[0], other(j))
    for h in (0, 1):
        end[0, h] = pair[h]
        for j in others:
            end[j, h] = send(pair[h], other(j))
        relay[h] = send(pair[h], centre_swap)
        for k in offsets:
            pair_across[k - 1][1 - h] = send(across[k - 1][1 - h], line_swap)
        for k in offsets:
            centre_across[k - 1][h] = send(centre[h], shift(k))
    for j in others:
        own[j, 1] = send(unit[1], other(j))

    def columns_of(parts):
        full = jnp.zeros((ngroups, cut + unit[1].shape[0], block), jnp.bfloat16)
        for (j, h), part in sorted(parts.items(), key=lambda item: item[0]):
            swapped = send(part, core_swap)
            for array, at in ((part, grp + j), (swapped, (grp ^ 1) + j)):
                full = lax.dynamic_update_slice(full, array[None], (at % ngroups, h * cut, 0))
        return full

    end_columns = columns_of(end)
    far_across = []
    for k in offsets:
        second = send(pair_across[k - 1][1], centre_swap)
        far_across.append([send(relay[0], shift(k)), second])

    def product(halves, cols):
        intersection = lax.dot_general(
            jnp.concatenate(halves, axis=0),
            cols,
            (((0,), (1,)), ((), ())),
            preferred_element_type=jnp.float32,
        )
        second = intersection * intersection
        return second * second

    def back(blocks):
        panels = [(product(b, end_columns) * SCALE).astype(jnp.float16) for b in blocks]
        return send(jnp.stack(panels), line_swap)

    first = [(centre, 3, 0)]
    second = [(relay, 2, 0)] + [(b, 3, k) for k, b in zip(offsets, centre_across)]
    third = [(b, 2, k) for k, b in zip(offsets, far_across)]
    returned = [(group, back([b for b, _, _ in group])) for group in (first, second, third)]
    columns = columns_of(own)

    out = jnp.zeros((ncolumns, block, ngroups, block), jnp.float32)

    def put(out, value, dz, k):
        at = (z ^ dz) * inner + (x + k) % inner
        return lax.dynamic_update_index_in_dim(out, value, at, 0)

    near = [(unit, 0, 0), (pair, 1, 0)]
    near += [(b, 0, k) for k, b in zip(offsets, across)]
    near += [(b, 1, k) for k, b in zip(offsets, pair_across)]
    for b, dz, k in near:
        out = put(out, product(b, columns), dz, k)
    for group, panels in returned:
        for i, (b, dz, k) in enumerate(group):
            mine = lax.optimization_barrier(product(b, columns))
            value = jnp.where(middle, mine, panels[i].astype(jnp.float32) * (1.0 / SCALE))
            out = put(out, value, jnp.where(middle, dz, dz ^ 1), k)
    return out.reshape(ncolumns * block, ngroups, block)


def plain(descriptors):
    squares = jnp.sum(descriptors * descriptors, axis=1, keepdims=True)
    unit = (descriptors * lax.rsqrt(squares + 1e-06)).astype(jnp.bfloat16)
    columns = lax.all_gather(unit, "grp", axis=0, tiled=True)
    rows = lax.all_gather(unit, "col", axis=0, tiled=True)
    intersection = jnp.dot(rows, columns.T, preferred_element_type=jnp.float32)
    second = intersection * intersection
    return (second * second).reshape(rows.shape[0], -1, unit.shape[0])


def solution(mesh):
    ngroups, ncolumns = mesh.shape["grp"], mesh.shape["col"]
    fits = ncolumns % LINE == 0 and ngroups % 2 == 0
    return jax.shard_map(
        shards if fits else plain,
        mesh=mesh,
        in_specs=(P(AXES, None),),
        out_specs=P("grp", None, "col"),
        check_vma=False,
    )
```

```python
import functools

import jax
import jax.numpy as jnp
from jax import lax
from jax.experimental import pallas as pl
from jax.experimental.pallas import tpu as pltpu
from jax.sharding import PartitionSpec as P


AXES = ("grp", "col")
LINE = 4
SCALE = 32768.0


HBM = pl.BlockSpec(memory_space=pl.ANY)
VMEM = pl.BlockSpec(memory_space=pltpu.VMEM)
SMEM = pl.BlockSpec(memory_space=pltpu.SMEM)


def unit_kernel(cut, data, first, second):
    squares = jnp.sum(data[...] * data[...], axis=0, keepdims=True)
    scale = lax.rsqrt(squares + 1e-06)
    first[...] = (data[:cut] * scale).astype(jnp.bfloat16)
    second[...] = (data[cut:] * scale).astype(jnp.bfloat16)


def normalize(data, cut):
    features, block = data.shape
    return pl.pallas_call(
        functools.partial(unit_kernel, cut),
        out_shape=[
            jax.ShapeDtypeStruct((cut, block), jnp.bfloat16),
            jax.ShapeDtypeStruct((features - cut, block), jnp.bfloat16),
        ],
        in_specs=[VMEM],
        out_specs=[VMEM, VMEM],
        cost_estimate=pl.CostEstimate(flops=0, bytes_accessed=6 * data.size, transcendentals=0),
        name="normalize",
    )(data)


def product_kernel(nparts, nblocks, cut, placed, *refs):
    slots, parts, refs = refs[0], refs[1 : 1 + 2 * nparts], refs[1 + 2 * nparts :]
    blocks, refs = refs[: 2 * nblocks], refs[2 * nblocks :]
    out, cols, rows, tile, sem_cols, sem_rows, sem_out = refs[-7:]
    size = rows.shape[2]

    def load(i, h, ref, dst, sem):
        span = pl.ds(0, cut) if h == 0 else pl.ds(cut, rows.shape[1] - cut)
        return pltpu.make_async_copy(ref, dst(span), sem.at[i, h])

    def column(i, h):
        at = pl.multiple_of(slots[i] * size, size)
        dst = lambda span: cols.at[span, pl.ds(at, size)]
        return load(i, h, parts[2 * i + h], dst, sem_cols)

    def row(i, h):
        return load(i, h, blocks[2 * i + h], lambda span: rows.at[i, span], sem_rows)

    def store(i):
        at = slots[nparts + i] if placed else i
        return pltpu.make_async_copy(tile.at[i], out.at[at], sem_out.at[i])

    for i in range(nparts):
        for h in (0, 1):
            column(i, h).start()
    for i in range(nblocks):
        for h in (0, 1):
            row(i, h).start()
    for i in range(nparts):
        for h in (0, 1):
            column(i, h).wait()
    for i in range(nblocks):
        for h in (0, 1):
            row(i, h).wait()
        value = lax.dot_general(
            rows[i], cols[...], (((0,), (0,)), ((), ())), preferred_element_type=jnp.float32
        )
        value = value * value
        value = value * value
        if placed:
            for a in range(nparts):
                tile[i, :, a, :] = value[:, a * size : (a + 1) * size]
        else:
            tile[i] = value * SCALE
        store(i).start()
    for i in range(nblocks):
        store(i).wait()


def products(blocks, parts, slots, out=None, shape=None):
    nparts, nblocks = len(parts), len(blocks)
    cut, size = blocks[0][0].shape
    features = cut + blocks[0][1].shape[0]
    placed = shape is not None
    operands = [slots] + [h for part in parts for h in part] + [h for b in blocks for h in b]
    alias = {}
    if out is not None:
        alias = {len(operands): 0}
        operands.append(out)
    panel = (size, nparts, size) if placed else (size, nparts * size)
    return pl.pallas_call(
        functools.partial(product_kernel, nparts, nblocks, cut, placed),
        out_shape=jax.ShapeDtypeStruct(shape if placed else (nblocks,) + panel, jnp.float32),
        in_specs=[SMEM] + [HBM] * (len(operands) - 1),
        out_specs=HBM,
        input_output_aliases=alias,
        scratch_shapes=[
            pltpu.VMEM((features, nparts * size), jnp.bfloat16),
            pltpu.VMEM((nblocks, features, size), jnp.bfloat16),
            pltpu.VMEM((nblocks,) + panel, jnp.float32),
            pltpu.SemaphoreType.DMA((nparts, 2)),
            pltpu.SemaphoreType.DMA((nblocks, 2)),
            pltpu.SemaphoreType.DMA((nblocks,)),
        ],
        cost_estimate=pl.CostEstimate(
            flops=2 * nblocks * size * features * nparts * size,
            bytes_accessed=2 * (nparts + nblocks) * features * size,
            transcendentals=0,
        ),
    )(*operands)


def place_kernel(count, slots, panels, old, out, tile, sem):
    del old
    size, nparts = tile.shape[1], tile.shape[2]

    def store(i):
        return pltpu.make_async_copy(tile.at[i], out.at[slots[i]], sem.at[i])

    @pl.when(slots[count] == 0)
    def _():
        for i in range(count):
            value = panels[i]
            for a in range(nparts):
                tile[i, :, a, :] = value[:, a * size : (a + 1) * size]
            store(i).start()
        for i in range(count):
            store(i).wait()


def place(panels, slots, out):
    count, size = panels.shape[:2]
    nparts = panels.shape[2] // size
    return pl.pallas_call(
        functools.partial(place_kernel, count),
        out_shape=jax.ShapeDtypeStruct(out.shape, out.dtype),
        in_specs=[SMEM, VMEM, HBM],
        out_specs=HBM,
        input_output_aliases={2: 0},
        scratch_shapes=[
            pltpu.VMEM((count, size, nparts, size), jnp.float32),
            pltpu.SemaphoreType.DMA((count,)),
        ],
        cost_estimate=pl.CostEstimate(flops=0, bytes_accessed=8 * panels.size, transcendentals=0),
        name="place",
    )(slots, panels, out)


def shards(descriptors):
    return exchange(descriptors)


def exchange(descriptors):
    ngroups = lax.axis_size("grp")
    ncolumns = lax.axis_size("col")
    block = descriptors.shape[0]
    inner = ncolumns // LINE
    offsets = range(1, inner)
    grp = lax.axis_index("grp")
    col = lax.axis_index("col")
    z, x = col // inner, col % inner
    middle = jnp.logical_or(z == 1, z == 2)

    def mid(zz):
        return zz in (1, 2)

    def send(array, move):
        pairs = []
        for g in range(ngroups):
            for c in range(ncolumns):
                tg, tz, tx = move(g, c // inner, c % inner)
                pairs.append((g * ncolumns + c, (tg * LINE + tz) * inner + tx % inner))
        return lax.ppermute(array, AXES, pairs)

    def line_swap(g, zz, xx):
        return g, zz ^ 1, xx

    def centre_swap(k):
        if k % inner == 0:
            return lambda g, zz, xx: (g, zz ^ 3, xx) if mid(zz) else (g ^ 1, zz, xx)
        return lambda g, zz, xx: (g, zz ^ 3, xx) if mid(zz) else (g, zz, xx - k)

    def shift(k, ends):
        if ends % inner == 0:
            return lambda g, zz, xx: (g, zz, xx - k) if mid(zz) else (g ^ 1, zz, xx)
        return lambda g, zz, xx: (g, zz, xx - (k if mid(zz) else ends))

    def other(j):
        return lambda g, zz, xx: ((g - j) % ngroups, zz, xx)

    def core_swap(g, zz, xx):
        return g ^ 1, zz, xx

    data = descriptors.T
    cut = data.shape[0] // 32 * 16
    unit = normalize(data, cut)
    others = range(2, ngroups, 2)
    halves = (0, 1)
    head, pair = [None, None], [None, None]
    across = [[None, None] for _ in offsets]
    own = {0: unit}
    for j in others:
        own[j] = [None, None]
    for h in halves:
        head[h] = send(unit[h], centre_swap(1))
        pair[h] = send(unit[h], line_swap)
        for k in offsets:
            across[k - 1][h] = send(unit[h], shift(k, k + 1))
        for j in others:
            own[j][h] = send(unit[h], other(j))
    relay, head_pair, end = [None, None], [None, None], {0: pair}
    across_pair = [[None, None] for _ in range(2, inner)]
    centre_across = [[None, None] for _ in offsets]
    for j in others:
        end[j] = [None, None]
    for h in halves:
        relay[h] = send(pair[h], centre_swap(inner - 1))
        for k in offsets:
            centre_across[k - 1][h] = send(head[h], shift(k, 0))
        head_pair[h] = send(head[h], line_swap)
        for k in range(2, inner):
            across_pair[k - 2][h] = send(across[k - 2][h], line_swap)
        for j in others:
            end[j][h] = send(pair[h], other(j))

    def with_cores(parts):
        full, at = [], []
        for j in sorted(parts):
            full += [parts[j], [send(part, core_swap) for part in parts[j]]]
            at += [(grp + j) % ngroups, ((grp ^ 1) + j) % ngroups]
        return full, at

    def slot(dz, k):
        return (z ^ dz) * inner + (x + k) % inner

    def where(for_middle, for_end):
        return jnp.where(middle, slot(*for_middle), slot(*for_end))

    def table(values):
        return jnp.stack([jnp.asarray(v, jnp.int32) for v in values])

    columns, columns_at = with_cores(own)
    shape = (ncolumns, block, ngroups, block)
    early = [(unit, slot(0, 0)), (pair, slot(1, 0)), (head, where((3, 0), (0, 1)))]
    for k in offsets:
        ends = (0, k + 1) if k + 1 < inner else (3, 0)
        early.append((across[k - 1], where((0, k), ends)))
    out = products(
        [b for b, _ in early], columns, table(columns_at + [at for _, at in early]), shape=shape,
    )
    end_columns, _ = with_cores(end)
    far_across = []
    for k in offsets:
        source = head_pair if k == 1 else across_pair[k - 2]
        second = send(source[1], centre_swap(0))
        far_across.append([send(relay[0], shift(k, 0)), second])

    def back(blocks):
        panels = products(blocks, end_columns, table(columns_at))
        return send(panels.astype(jnp.float16), line_swap)

    returned = [back([relay] + centre_across), back(far_across)]
    late = [(head_pair, where((1, 1), (2, 0))), (relay, where((2, 0), (1, inner - 1)))]
    for k in range(2, inner):
        late.append((across_pair[k - 2], where((1, k), (1, k - 1))))
    late += [(b, where((3, k), (2, k))) for k, b in zip(offsets, centre_across)]
    late += [(b, where((2, k), (3, k))) for k, b in zip(offsets, far_across)]
    out = products(
        [b for b, _ in late], columns, table(columns_at + [at for _, at in late]), out=out,
        shape=shape,
    )
    panels = jnp.concatenate(returned).astype(jnp.float32) * (1.0 / SCALE)
    slots = [slot(3, 0)] + [slot(2, k) for k in offsets] + [slot(3, k) for k in offsets]
    out = place(panels, table(slots + [middle]), out)
    return out.reshape(ncolumns * block, ngroups, block)


def plain(descriptors):
    squares = jnp.sum(descriptors * descriptors, axis=1, keepdims=True)
    unit = (descriptors * lax.rsqrt(squares + 1e-06)).astype(jnp.bfloat16)
    columns = lax.all_gather(unit, "grp", axis=0, tiled=True)
    rows = lax.all_gather(unit, "col", axis=0, tiled=True)
    intersection = jnp.dot(rows, columns.T, preferred_element_type=jnp.float32)
    second = intersection * intersection
    return (second * second).reshape(rows.shape[0], -1, unit.shape[0])


def solution(mesh):
    ngroups, ncolumns = mesh.shape["grp"], mesh.shape["col"]
    fits = ncolumns % (2 * LINE) == 0 and ngroups % 2 == 0
    return jax.shard_map(
        shards if fits else plain,
        mesh=mesh,
        in_specs=(P(AXES, None),),
        out_specs=P("grp", None, "col"),
        check_vma=False,
    )
```

```python
import functools

import jax
import jax.numpy as jnp
from jax import lax
from jax.experimental import pallas as pl
from jax.experimental.pallas import tpu as pltpu
from jax.sharding import PartitionSpec as P


AXES = ("grp", "col")
LINE = 4
SCALE = 32768.0


VMEM = pl.BlockSpec(memory_space=pltpu.VMEM)


def unit_kernel(cut, data, first, second):
    squares = jnp.sum(data[...] * data[...], axis=0, keepdims=True)
    scale = lax.rsqrt(squares + 1e-06)
    first[...] = (data[:cut] * scale).astype(jnp.bfloat16)
    second[...] = (data[cut:] * scale).astype(jnp.bfloat16)


def normalize(data, cut):
    features, block = data.shape
    return pl.pallas_call(
        functools.partial(unit_kernel, cut),
        out_shape=[
            jax.ShapeDtypeStruct((cut, block), jnp.bfloat16),
            jax.ShapeDtypeStruct((features - cut, block), jnp.bfloat16),
        ],
        in_specs=[VMEM],
        out_specs=[VMEM, VMEM],
        cost_estimate=pl.CostEstimate(flops=0, bytes_accessed=6 * data.size, transcendentals=0),
        name="normalize",
    )(data)


def shards(descriptors):
    return exchange(descriptors)


def exchange(descriptors):
    ngroups = lax.axis_size("grp")
    ncolumns = lax.axis_size("col")
    block = descriptors.shape[0]
    inner = ncolumns // LINE
    offsets = range(1, inner)
    grp = lax.axis_index("grp")
    col = lax.axis_index("col")
    z, x = col // inner, col % inner
    middle = jnp.logical_or(z == 1, z == 2)

    def mid(zz):
        return zz in (1, 2)

    def send(array, move):
        pairs = []
        for g in range(ngroups):
            for c in range(ncolumns):
                tg, tz, tx = move(g, c // inner, c % inner)
                pairs.append((g * ncolumns + c, (tg * LINE + tz) * inner + tx % inner))
        return lax.ppermute(array, AXES, pairs)

    def line_swap(g, zz, xx):
        return g, zz ^ 1, xx

    def centre_swap(k):
        if k % inner == 0:
            return lambda g, zz, xx: (g, zz ^ 3, xx) if mid(zz) else (g ^ 1, zz, xx)
        return lambda g, zz, xx: (g, zz ^ 3, xx) if mid(zz) else (g, zz, xx - k)

    def shift(k, ends):
        if ends % inner == 0:
            return lambda g, zz, xx: (g, zz, xx - k) if mid(zz) else (g ^ 1, zz, xx)
        return lambda g, zz, xx: (g, zz, xx - (k if mid(zz) else ends))

    def other(j):
        return lambda g, zz, xx: ((g - j) % ngroups, zz, xx)

    def core_swap(g, zz, xx):
        return g ^ 1, zz, xx

    data = descriptors.T
    cut = data.shape[0] // 32 * 16
    unit = normalize(data, cut)
    others = range(2, ngroups, 2)
    halves = (0, 1)
    head, pair = [None, None], [None, None]
    across = [[None, None] for _ in offsets]
    own = {0: unit}
    for j in others:
        own[j] = [None, None]
    for h in halves:
        head[h] = send(unit[h], centre_swap(1))
        pair[h] = send(unit[h], line_swap)
        for k in offsets:
            across[k - 1][h] = send(unit[h], shift(k, k + 1))
        for j in others:
            own[j][h] = send(unit[h], other(j))
    relay, head_pair, end = [None, None], [None, None], {0: pair}
    across_pair = [[None, None] for _ in range(2, inner)]
    centre_across = [[None, None] for _ in offsets]
    for j in others:
        end[j] = [None, None]
    for h in halves:
        relay[h] = send(pair[h], centre_swap(inner - 1))
        for k in offsets:
            centre_across[k - 1][h] = send(head[h], shift(k, 0))
        head_pair[h] = send(head[h], line_swap)
        for k in range(2, inner):
            across_pair[k - 2][h] = send(across[k - 2][h], line_swap)
        for j in others:
            end[j][h] = send(pair[h], other(j))

    def columns_of(parts):
        full = jnp.zeros((ngroups,) + data.shape, jnp.bfloat16)
        for j in sorted(parts):
            for h in halves:
                part = parts[j][h]
                swapped = send(part, core_swap)
                for array, at in ((part, grp + j), (swapped, (grp ^ 1) + j)):
                    start = (at % ngroups, h * cut, 0)
                    full = lax.dynamic_update_slice(full, array[None], start)
        return full

    def slot(dz, k):
        return (z ^ dz) * inner + (x + k) % inner

    def where(for_middle, for_end):
        return jnp.where(middle, slot(*for_middle), slot(*for_end))

    def fourth(block, cols):
        intersection = lax.dot_general(
            jnp.concatenate(block, axis=0),
            cols,
            (((0,), (1,)), ((), ())),
            preferred_element_type=jnp.float32,
        )
        second = intersection * intersection
        return second * second

    def product(block, cols):
        return lax.optimization_barrier(fourth(block, cols))

    def put(out, value, at):
        return lax.dynamic_update_index_in_dim(out, value, at, 0)

    columns = columns_of(own)
    early = [(unit, slot(0, 0)), (pair, slot(1, 0)), (head, where((3, 0), (0, 1)))]
    for k in offsets:
        ends = (0, k + 1) if k + 1 < inner else (3, 0)
        early.append((across[k - 1], where((0, k), ends)))
    out = jnp.zeros((ncolumns, block, ngroups, block), jnp.float32)
    for b, at in early:
        out = put(out, product(b, columns), at)
    end_columns = columns_of(end)
    far_across = []
    for k in offsets:
        source = head_pair if k == 1 else across_pair[k - 2]
        second = send(source[1], centre_swap(0))
        far_across.append([send(relay[0], shift(k, 0)), second])

    def back(blocks):
        panels = [(fourth(b, end_columns) * SCALE).astype(jnp.float16) for b in blocks]
        return send(jnp.stack(panels), line_swap)

    returned = back([relay] + centre_across)
    returned_far = back(far_across)
    late = [(head_pair, where((1, 1), (2, 0))), (relay, where((2, 0), (1, inner - 1)))]
    for k in range(2, inner):
        late.append((across_pair[k - 2], where((1, k), (1, k - 1))))
    late += [(b, where((3, k), (2, k))) for k, b in zip(offsets, centre_across)]
    for b, at in late:
        out = put(out, product(b, columns), at)
    for k, b in zip(offsets, far_across):
        out = put(out, product(b, columns), where((2, k), (3, k)))
    slots = [slot(3, 0)] + [slot(2, k) for k in offsets] + [slot(3, k) for k in offsets]
    panels = [returned[i] for i in range(inner)] + [returned_far[k - 1] for k in offsets]
    for at, panel in zip(slots, panels):
        old = lax.dynamic_index_in_dim(out, at, 0, keepdims=False)
        out = put(out, jnp.where(middle, old, panel.astype(jnp.float32) * (1.0 / SCALE)), at)
    return out.reshape(ncolumns * block, ngroups, block)


def plain(descriptors):
    squares = jnp.sum(descriptors * descriptors, axis=1, keepdims=True)
    unit = (descriptors * lax.rsqrt(squares + 1e-06)).astype(jnp.bfloat16)
    columns = lax.all_gather(unit, "grp", axis=0, tiled=True)
    rows = lax.all_gather(unit, "col", axis=0, tiled=True)
    intersection = jnp.dot(rows, columns.T, preferred_element_type=jnp.float32)
    second = intersection * intersection
    return (second * second).reshape(rows.shape[0], -1, unit.shape[0])


def solution(mesh):
    ngroups, ncolumns = mesh.shape["grp"], mesh.shape["col"]
    fits = ncolumns % (2 * LINE) == 0 and ngroups % 2 == 0
    return jax.shard_map(
        shards if fits else plain,
        mesh=mesh,
        in_specs=(P(AXES, None),),
        out_specs=P("grp", None, "col"),
        check_vma=False,
    )
```

```python
import functools

import jax
import jax.numpy as jnp
from jax import lax
from jax.experimental import pallas as pl
from jax.experimental.pallas import tpu as pltpu
from jax.sharding import PartitionSpec as P


AXES = ("grp", "col")
LINE = 4
SCALE = 32768.0


VMEM = pl.BlockSpec(memory_space=pltpu.VMEM)


def unit_kernel(cut, data, first, second):
    squares = jnp.sum(data[...] * data[...], axis=0, keepdims=True)
    scale = lax.rsqrt(squares + 1e-06)
    first[...] = (data[:cut] * scale).astype(jnp.bfloat16)
    second[...] = (data[cut:] * scale).astype(jnp.bfloat16)


def normalize(data, cut):
    features, block = data.shape
    return pl.pallas_call(
        functools.partial(unit_kernel, cut),
        out_shape=[
            jax.ShapeDtypeStruct((cut, block), jnp.bfloat16),
            jax.ShapeDtypeStruct((features - cut, block), jnp.bfloat16),
        ],
        in_specs=[VMEM],
        out_specs=[VMEM, VMEM],
        cost_estimate=pl.CostEstimate(flops=0, bytes_accessed=6 * data.size, transcendentals=0),
        compiler_params=pltpu.CompilerParams(vmem_limit_bytes=8 * data.size),
        name="normalize",
    )(data)


def shards(descriptors):
    return exchange(descriptors)


def exchange(descriptors):
    ngroups = lax.axis_size("grp")
    ncolumns = lax.axis_size("col")
    block = descriptors.shape[0]
    inner = ncolumns // LINE
    offsets = range(1, inner)
    others = range(2, ngroups, 2)
    halves = (0, 1)
    grp = lax.axis_index("grp")
    col = lax.axis_index("col")
    z, x = col // inner, col % inner
    middle = jnp.logical_or(z == 1, z == 2)

    def slot(dz, k):
        return (z ^ dz) * inner + (x + k) % inner

    def where(for_middle, for_end):
        return jnp.where(middle, slot(*for_middle), slot(*for_end))

    indices = {("own", j): (grp + j) % ngroups for j in range(0, ngroups, 2)}
    indices.update({("swapped", j): ((grp ^ 1) + j) % ngroups for j in range(0, ngroups, 2)})
    indices.update({"unit": slot(0, 0), "pair": slot(1, 0), "head": where((3, 0), (0, 1))})
    indices.update({"head_pair": where((1, 1), (2, 0)), "relay": where((2, 0), (1, inner - 1))})
    indices.update({("across", k): where((0, k), (0, k + 1)) for k in range(1, inner - 1)})
    indices.update({("across_pair", k): where((1, k), (1, k - 1)) for k in range(2, inner)})
    indices["back", 0] = where((0, inner - 1), (3, 0))
    indices.update({("back", k): where((3, k), (2, k)) for k in offsets})
    indices.update({("far", k): where((2, k), (3, k)) for k in offsets})
    names = list(indices)
    held = lax.optimization_barrier((descriptors, middle) + tuple(indices[n] for n in names))
    descriptors, middle = held[:2]
    at = dict(zip(names, held[2:]))

    def mid(zz):
        return zz in (1, 2)

    def send(array, move):
        pairs = []
        for g in range(ngroups):
            for c in range(ncolumns):
                tg, tz, tx = move(g, c // inner, c % inner)
                pairs.append((g * ncolumns + c, (tg * LINE + tz) * inner + tx % inner))
        return lax.ppermute(array, AXES, pairs)

    def line_swap(g, zz, xx):
        return g, zz ^ 1, xx

    def centre_swap(k):
        if k % inner == 0:
            return lambda g, zz, xx: (g, zz ^ 3, xx) if mid(zz) else (g ^ 1, zz, xx)
        return lambda g, zz, xx: (g, zz ^ 3, xx) if mid(zz) else (g, zz, xx - k)

    def shift(k, ends):
        if ends % inner == 0:
            return lambda g, zz, xx: (g, zz, xx - k) if mid(zz) else (g ^ 1, zz, xx)
        return lambda g, zz, xx: (g, zz, xx - (k if mid(zz) else ends))

    def other(j):
        return lambda g, zz, xx: ((g - j) % ngroups, zz, xx)

    def core_swap(g, zz, xx):
        return g ^ 1, zz, xx

    data = descriptors.T
    cut = data.shape[0] // 32 * 16
    unit = normalize(data, cut)
    head, pair = [None, None], [None, None]
    across = [[None, None] for _ in offsets]
    own = {0: unit}
    for j in others:
        own[j] = [None, None]
    for h in halves:
        head[h] = send(unit[h], centre_swap(1))
        pair[h] = send(unit[h], line_swap)
        for k in offsets:
            across[k - 1][h] = send(unit[h], shift(k, k + 1))
        for j in others:
            own[j][h] = send(unit[h], other(j))
    relay, head_pair, end = [None, None], [None, None], {0: pair}
    across_pair = [[None, None] for _ in range(2, inner)]
    centre_across = [[None, None] for _ in offsets]
    for j in others:
        end[j] = [None, None]
    for h in halves:
        relay[h] = send(pair[h], centre_swap(inner - 1))
        for k in offsets:
            centre_across[k - 1][h] = send(head[h], shift(k, 0))
        head_pair[h] = send(head[h], line_swap)
        for k in range(2, inner):
            across_pair[k - 2][h] = send(across[k - 2][h], line_swap)
        for j in others:
            end[j][h] = send(pair[h], other(j))

    def columns_of(parts):
        full = jnp.zeros((ngroups,) + data.shape, jnp.bfloat16)
        for j in sorted(parts):
            for h in halves:
                part = parts[j][h]
                swapped = send(part, core_swap)
                for array, index in ((part, at["own", j]), (swapped, at["swapped", j])):
                    full = lax.dynamic_update_slice(
                        full, array[None], (index, h * cut, 0), allow_negative_indices=False
                    )
        return full

    def fourth(block, cols):
        intersection = lax.dot_general(
            jnp.concatenate(block, axis=0),
            cols,
            (((0,), (1,)), ((), ())),
            preferred_element_type=jnp.float32,
        )
        second = intersection * intersection
        return second * second

    def product(block):
        return lax.optimization_barrier(fourth(block, columns))

    def put(out, value, index):
        return lax.dynamic_update_index_in_dim(
            out, value, index, 0, allow_negative_indices=False
        )

    columns = columns_of(own)
    out = jnp.zeros((ncolumns, block, ngroups, block), jnp.float32)
    out = put(out, product(unit), at["unit"])
    out = put(out, product(pair), at["pair"])
    out = put(out, product(head), at["head"])
    for k in range(1, inner - 1):
        out = put(out, product(across[k - 1]), at["across", k])
    mine = [product(across[-1])]
    end_columns = columns_of(end)
    far_across = []
    for k in offsets:
        source = head_pair if k == 1 else across_pair[k - 2]
        second = send(source[1], centre_swap(0))
        far_across.append([send(relay[0], shift(k, 0)), second])

    def back(blocks):
        panels = [(fourth(b, end_columns) * SCALE).astype(jnp.float16) for b in blocks]
        return send(jnp.stack(panels), line_swap)

    returned = back([relay] + centre_across)
    returned_far = back(far_across)
    out = put(out, product(head_pair), at["head_pair"])
    out = put(out, product(relay), at["relay"])
    for k in range(2, inner):
        out = put(out, product(across_pair[k - 2]), at["across_pair", k])
    mine += [product(b) for b in centre_across]
    mine += [product(b) for b in far_across]
    slots = [at["back", k] for k in range(inner)] + [at["far", k] for k in offsets]
    panels = [returned[k] for k in range(inner)] + [returned_far[k - 1] for k in offsets]
    for index, panel, value in zip(slots, panels, mine):
        theirs = panel.astype(jnp.float32) * (1.0 / SCALE)
        out = put(out, jnp.where(middle, value, theirs), index)
    return out.reshape(ncolumns * block, ngroups, block)


def plain(descriptors):
    squares = jnp.sum(descriptors * descriptors, axis=1, keepdims=True)
    unit = (descriptors * lax.rsqrt(squares + 1e-06)).astype(jnp.bfloat16)
    columns = lax.all_gather(unit, "grp", axis=0, tiled=True)
    rows = lax.all_gather(unit, "col", axis=0, tiled=True)
    intersection = jnp.dot(rows, columns.T, preferred_element_type=jnp.float32)
    second = intersection * intersection
    return (second * second).reshape(rows.shape[0], -1, unit.shape[0])


def solution(mesh):
    ngroups, ncolumns = mesh.shape["grp"], mesh.shape["col"]
    fits = ncolumns % (2 * LINE) == 0 and ngroups % 2 == 0
    return jax.shard_map(
        shards if fits else plain,
        mesh=mesh,
        in_specs=(P(AXES, None),),
        out_specs=P("grp", None, "col"),
        check_vma=False,
    )
```

```python
import functools

import jax
import jax.numpy as jnp
from jax import lax
from jax.experimental import pallas as pl
from jax.experimental.pallas import tpu as pltpu
from jax.sharding import PartitionSpec as P


AXES = ("grp", "col")
LINE = 4
SCALE = 32768.0


VMEM = pl.BlockSpec(memory_space=pltpu.VMEM)


def unit_kernel(cut, data, first, second):
    squares = jnp.sum(data[...] * data[...], axis=0, keepdims=True)
    scale = lax.rsqrt(squares + 1e-06)
    first[...] = (data[:cut] * scale).astype(jnp.bfloat16)
    second[...] = (data[cut:] * scale).astype(jnp.bfloat16)


def normalize(data, cut):
    features, block = data.shape
    return pl.pallas_call(
        functools.partial(unit_kernel, cut),
        out_shape=[
            jax.ShapeDtypeStruct((cut, block), jnp.bfloat16),
            jax.ShapeDtypeStruct((features - cut, block), jnp.bfloat16),
        ],
        in_specs=[VMEM],
        out_specs=[VMEM, VMEM],
        cost_estimate=pl.CostEstimate(flops=0, bytes_accessed=6 * data.size, transcendentals=0),
        compiler_params=pltpu.CompilerParams(vmem_limit_bytes=8 * data.size),
        name="normalize",
    )(data)


def shards(descriptors):
    return exchange(descriptors)


def exchange(descriptors):
    ngroups = lax.axis_size("grp")
    ncolumns = lax.axis_size("col")
    block = descriptors.shape[0]
    inner = ncolumns // LINE
    offsets = range(1, inner)
    others = range(2, ngroups, 2)
    halves = (0, 1)
    grp = lax.axis_index("grp")
    col = lax.axis_index("col")
    z, x = col // inner, col % inner
    middle = jnp.logical_or(z == 1, z == 2)

    def slot(dz, k):
        return (z ^ dz) * inner + (x + k) % inner

    def where(for_middle, for_end):
        return jnp.where(middle, slot(*for_middle), slot(*for_end))

    indices = {("own", j): (grp + j) % ngroups for j in range(0, ngroups, 2)}
    indices.update({("swapped", j): ((grp ^ 1) + j) % ngroups for j in range(0, ngroups, 2)})
    indices.update({"unit": slot(0, 0), "pair": slot(1, 0), "head": where((3, 0), (0, 1))})
    indices.update({"head_pair": where((1, 1), (2, 0)), "relay": where((2, 0), (1, inner - 1))})
    indices.update({("across", k): where((0, k), (0, k + 1)) for k in range(1, inner - 1)})
    indices.update({("across_pair", k): where((1, k), (1, k - 1)) for k in range(2, inner)})
    indices["back", 0] = where((0, inner - 1), (3, 0))
    indices.update({("back", k): where((3, k), (2, k)) for k in offsets})
    indices.update({("far", k): where((2, k), (3, k)) for k in offsets})
    names = list(indices)
    held = lax.optimization_barrier((descriptors, middle) + tuple(indices[n] for n in names))
    descriptors, middle = held[:2]
    at = dict(zip(names, held[2:]))

    def mid(zz):
        return zz in (1, 2)

    def send(array, move):
        pairs = []
        for g in range(ngroups):
            for c in range(ncolumns):
                tg, tz, tx = move(g, c // inner, c % inner)
                pairs.append((g * ncolumns + c, (tg * LINE + tz) * inner + tx % inner))
        return lax.ppermute(array, AXES, pairs)

    def line_swap(g, zz, xx):
        return g, zz ^ 1, xx

    def centre_swap(k):
        if k % inner == 0:
            return lambda g, zz, xx: (g, zz ^ 3, xx) if mid(zz) else (g ^ 1, zz, xx)
        return lambda g, zz, xx: (g, zz ^ 3, xx) if mid(zz) else (g, zz, xx - k)

    def shift(k, ends):
        if ends % inner == 0:
            return lambda g, zz, xx: (g, zz, xx - k) if mid(zz) else (g ^ 1, zz, xx)
        return lambda g, zz, xx: (g, zz, xx - (k if mid(zz) else ends))

    def other(j):
        return lambda g, zz, xx: ((g - j) % ngroups, zz, xx)

    def core_swap(g, zz, xx):
        return g ^ 1, zz, xx

    data = descriptors.T
    cut = data.shape[0] // 32 * 16
    unit = normalize(data, cut)
    head, pair, relay, head_pair = ([None, None] for _ in range(4))
    across, centre_across = ([[None, None] for _ in offsets] for _ in range(2))
    across_pair = [[None, None] for _ in range(2, inner)]
    own, end = {0: unit}, {0: pair}
    for j in others:
        own[j], end[j] = [None, None], [None, None]
    for h in halves:
        head[h] = send(unit[h], centre_swap(1))
        for k in offsets:
            across[k - 1][h] = send(unit[h], shift(k, k + 1))
        pair[h] = send(unit[h], line_swap)
        if h == 0:
            for j in others:
                own[j][h] = send(unit[h], other(j))
    swapped = {("own", 0, h): send(unit[h], core_swap) for h in halves}
    for h in halves:
        for j in others:
            end[j][h] = send(pair[h], other(j))
        relay[h] = send(pair[h], centre_swap(inner - 1))
        for k in offsets:
            centre_across[k - 1][h] = send(head[h], shift(k, 0))
        head_pair[h] = send(head[h], line_swap)
        for k in range(2, inner):
            across_pair[k - 2][h] = send(across[k - 2][h], line_swap)
    for j in others:
        own[j][1] = send(unit[1], other(j))
    for j in others:
        swapped["own", j, 0] = send(own[j][0], core_swap)
    swapped.update({("end", 0, h): send(pair[h], core_swap) for h in halves})
    for j in others:
        swapped["end", j, 0] = send(end[j][0], core_swap)
    far_across = [[send(head_pair[0] if k == 1 else across_pair[k - 2][0], centre_swap(0)), None] for k in offsets]
    for j in others:
        swapped["end", j, 1] = send(end[j][1], core_swap)
    for k in offsets:
        far_across[k - 1][1] = send(relay[1], shift(k, 0))

    def columns_of(name, parts):
        full = jnp.zeros((ngroups,) + data.shape, jnp.bfloat16)
        for j in sorted(parts):
            for h in halves:
                pieces = ((parts[j][h], at["own", j]), (swapped[name, j, h], at["swapped", j]))
                for array, index in pieces:
                    full = lax.dynamic_update_slice(
                        full, array[None], (index, h * cut, 0), allow_negative_indices=False
                    )
        return full

    def fourth(block, cols):
        intersection = lax.dot_general(
            jnp.concatenate(block, axis=0),
            cols,
            (((0,), (1,)), ((), ())),
            preferred_element_type=jnp.float32,
        )
        second = intersection * intersection
        return second * second

    def product(block):
        return lax.optimization_barrier(fourth(block, columns))

    def put(out, value, index):
        return lax.dynamic_update_index_in_dim(
            out, value, index, 0, allow_negative_indices=False
        )

    def back(block):
        panel = (fourth(block, end_columns) * SCALE).astype(jnp.float16)
        return send(panel, line_swap)

    end_columns = columns_of("end", end)
    panels = [back(b) for b in [relay] + centre_across]
    for j in others:
        swapped["own", j, 1] = send(own[j][1], core_swap)
    columns = columns_of("own", own)
    out = jnp.zeros((ncolumns, block, ngroups, block), jnp.float32)
    out = put(out, product(unit), at["unit"])
    out = put(out, product(pair), at["pair"])
    out = put(out, product(head), at["head"])
    for k in range(1, inner - 1):
        out = put(out, product(across[k - 1]), at["across", k])
    mine = [product(across[-1])]
    panels += [back(b) for b in far_across]
    out = put(out, product(head_pair), at["head_pair"])
    out = put(out, product(relay), at["relay"])
    for k in range(2, inner):
        out = put(out, product(across_pair[k - 2]), at["across_pair", k])
    mine += [product(b) for b in centre_across + far_across]
    slots = [at["back", k] for k in range(inner)] + [at["far", k] for k in offsets]
    for index, panel, value in zip(slots, panels, mine):
        theirs = panel.astype(jnp.float32) * (1.0 / SCALE)
        out = put(out, jnp.where(middle, value, theirs), index)
    return out.reshape(ncolumns * block, ngroups, block)


def plain(descriptors):
    squares = jnp.sum(descriptors * descriptors, axis=1, keepdims=True)
    unit = (descriptors * lax.rsqrt(squares + 1e-06)).astype(jnp.bfloat16)
    columns = lax.all_gather(unit, "grp", axis=0, tiled=True)
    rows = lax.all_gather(unit, "col", axis=0, tiled=True)
    intersection = jnp.dot(rows, columns.T, preferred_element_type=jnp.float32)
    second = intersection * intersection
    return (second * second).reshape(rows.shape[0], -1, unit.shape[0])


def solution(mesh):
    ngroups, ncolumns = mesh.shape["grp"], mesh.shape["col"]
    fits = ncolumns % (2 * LINE) == 0 and ngroups % 2 == 0
    return jax.shard_map(
        shards if fits else plain,
        mesh=mesh,
        in_specs=(P(AXES, None),),
        out_specs=P("grp", None, "col"),
        check_vma=False,
    )
```

```python
import functools

import jax
import jax.numpy as jnp
from jax import lax
from jax.experimental import pallas as pl
from jax.experimental.pallas import tpu as pltpu
from jax.sharding import PartitionSpec as P


AXES = ("grp", "col")
LINE = 4
SCALE = 32768.0


VMEM = pl.BlockSpec(memory_space=pltpu.VMEM)


def unit_kernel(cut, chunks, source, first, second, data, sems):
    size = data.shape[0] // chunks

    def load(i):
        span = pl.ds(i * size, size)
        return pltpu.make_async_copy(source.at[span], data.at[span], sems.at[i])

    for i in range(chunks):
        load(i).start()
    squares = jnp.zeros((1, data.shape[1]), jnp.float32)
    for i in range(chunks):
        load(i).wait()
        part = data[i * size : (i + 1) * size]
        squares += jnp.sum(part * part, axis=0, keepdims=True)
    scale = lax.rsqrt(squares + 1e-06)
    first[...] = (data[:cut] * scale).astype(jnp.bfloat16)
    second[...] = (data[cut:] * scale).astype(jnp.bfloat16)


def normalize(data, cut):
    features, block = data.shape
    chunks = next(n for n in (5, 4, 3, 2, 1) if features % (8 * n) == 0)
    return pl.pallas_call(
        functools.partial(unit_kernel, cut, chunks),
        out_shape=[
            jax.ShapeDtypeStruct((cut, block), jnp.bfloat16),
            jax.ShapeDtypeStruct((features - cut, block), jnp.bfloat16),
        ],
        in_specs=[pl.BlockSpec(memory_space=pltpu.HBM)],
        out_specs=[VMEM, VMEM],
        scratch_shapes=[
            pltpu.VMEM((features, block), jnp.float32),
            pltpu.SemaphoreType.DMA((chunks,)),
        ],
        cost_estimate=pl.CostEstimate(flops=0, bytes_accessed=6 * data.size, transcendentals=0),
        compiler_params=pltpu.CompilerParams(vmem_limit_bytes=16 * data.size),
        name="normalize",
    )(data)


def shards(descriptors):
    return exchange(descriptors)


def exchange(descriptors):
    ngroups = lax.axis_size("grp")
    ncolumns = lax.axis_size("col")
    block = descriptors.shape[0]
    inner = ncolumns // LINE
    offsets = range(1, inner)
    others = range(2, ngroups, 2)
    halves = (0, 1)
    grp = lax.axis_index("grp")
    col = lax.axis_index("col")
    z, x = col // inner, col % inner
    middle = jnp.logical_or(z == 1, z == 2)

    def slot(dz, k):
        return (z ^ dz) * inner + (x + k) % inner

    def where(for_middle, for_end):
        return jnp.where(middle, slot(*for_middle), slot(*for_end))

    indices = {("own", j): (grp + j) % ngroups for j in range(0, ngroups, 2)}
    indices.update({("swapped", j): ((grp ^ 1) + j) % ngroups for j in range(0, ngroups, 2)})
    indices.update({"unit": slot(0, 0), "pair": slot(1, 0), "head": where((3, 0), (0, 1))})
    indices.update({"head_pair": where((1, 1), (2, 0)), "relay": where((2, 0), (1, inner - 1))})
    indices.update({("across", k): where((0, k), (0, k + 1)) for k in range(1, inner - 1)})
    indices.update({("across_pair", k): where((1, k), (1, k - 1)) for k in range(2, inner)})
    indices["back", 0] = where((0, inner - 1), (3, 0))
    indices.update({("back", k): where((3, k), (2, k)) for k in offsets})
    indices.update({("far", k): where((2, k), (3, k)) for k in offsets})
    names = list(indices)
    held = lax.optimization_barrier((descriptors, middle) + tuple(indices[n] for n in names))
    descriptors, middle = held[:2]
    at = dict(zip(names, held[2:]))

    def mid(zz):
        return zz in (1, 2)

    def send(array, move):
        pairs = []
        for g in range(ngroups):
            for c in range(ncolumns):
                tg, tz, tx = move(g, c // inner, c % inner)
                pairs.append((g * ncolumns + c, (tg * LINE + tz) * inner + tx % inner))
        return lax.ppermute(array, AXES, pairs)

    def line_swap(g, zz, xx):
        return g, zz ^ 1, xx

    def centre_swap(k):
        if k % inner == 0:
            return lambda g, zz, xx: (g, zz ^ 3, xx) if mid(zz) else (g ^ 1, zz, xx)
        return lambda g, zz, xx: (g, zz ^ 3, xx) if mid(zz) else (g, zz, xx - k)

    def shift(k, ends):
        if ends % inner == 0:
            return lambda g, zz, xx: (g, zz, xx - k) if mid(zz) else (g ^ 1, zz, xx)
        return lambda g, zz, xx: (g, zz, xx - (k if mid(zz) else ends))

    def other(j):
        return lambda g, zz, xx: ((g - j) % ngroups, zz, xx)

    def core_swap(g, zz, xx):
        return g ^ 1, zz, xx

    data = descriptors.T
    cut = data.shape[0] // 32 * 16
    unit = normalize(data, cut)
    head, pair, relay, head_pair = ([None, None] for _ in range(4))
    across, centre_across = ([[None, None] for _ in offsets] for _ in range(2))
    across_pair = [[None, None] for _ in range(2, inner)]
    own, end = {0: unit}, {0: pair}
    for j in others:
        own[j], end[j] = [None, None], [None, None]
    for h in halves:
        head[h] = send(unit[h], centre_swap(1))
        for k in offsets:
            across[k - 1][h] = send(unit[h], shift(k, k + 1))
        pair[h] = send(unit[h], line_swap)
        for j in others:
            own[j][h] = send(unit[h], other(j))
    swapped = {("own", 0, h): send(unit[h], core_swap) for h in halves}
    for h in halves:
        for j in others:
            end[j][h] = send(pair[h], other(j))
        relay[h] = send(pair[h], centre_swap(inner - 1))
        for k in offsets:
            centre_across[k - 1][h] = send(head[h], shift(k, 0))
        head_pair[h] = send(head[h], line_swap)
        for k in range(2, inner):
            across_pair[k - 2][h] = send(across[k - 2][h], line_swap)
    for j in others:
        swapped.update({("own", j, h): send(own[j][h], core_swap) for h in halves})
    swapped.update({("end", 0, h): send(pair[h], core_swap) for h in halves})
    for j in others:
        swapped["end", j, 0] = send(end[j][0], core_swap)
    far_across = [[None, None] for _ in offsets]
    for k in offsets:
        source = head_pair if k == 1 else across_pair[k - 2]
        far_across[k - 1][0] = send(source[0], centre_swap(0))
    for j in others:
        swapped["end", j, 1] = send(end[j][1], core_swap)
    for k in offsets:
        far_across[k - 1][1] = send(relay[1], shift(k, 0))

    def columns_of(name, parts):
        full = jnp.zeros((ngroups,) + data.shape, jnp.bfloat16)
        for j in sorted(parts):
            for h in halves:
                pieces = ((parts[j][h], at["own", j]), (swapped[name, j, h], at["swapped", j]))
                for array, index in pieces:
                    full = lax.dynamic_update_slice(
                        full, array[None], (index, h * cut, 0), allow_negative_indices=False
                    )
        return full

    def fourth(block, cols):
        intersection = lax.dot_general(
            jnp.concatenate(block, axis=0),
            cols,
            (((0,), (1,)), ((), ())),
            preferred_element_type=jnp.float32,
        )
        second = intersection * intersection
        return second * second

    def product(block):
        return lax.optimization_barrier(fourth(block, columns))

    def put(out, value, index):
        return lax.dynamic_update_index_in_dim(
            out, value, index, 0, allow_negative_indices=False
        )

    def back(block):
        panel = (fourth(block, end_columns) * SCALE).astype(jnp.float16)
        return send(panel, line_swap)

    columns = columns_of("own", own)
    out = jnp.zeros((ncolumns, block, ngroups, block), jnp.float32)
    out = put(out, product(unit), at["unit"])
    out = put(out, product(pair), at["pair"])
    out = put(out, product(head), at["head"])
    for k in range(1, inner - 1):
        out = put(out, product(across[k - 1]), at["across", k])
    mine = [product(across[-1])]
    end_columns = columns_of("end", end)
    panels = [back(b) for b in [relay] + centre_across]
    out = put(out, product(head_pair), at["head_pair"])
    out = put(out, product(relay), at["relay"])
    for k in range(2, inner):
        out = put(out, product(across_pair[k - 2]), at["across_pair", k])
    mine += [product(b) for b in centre_across]
    panels += [back(b) for b in far_across]
    mine += [product(b) for b in far_across]
    slots = [at["back", k] for k in range(inner)] + [at["far", k] for k in offsets]
    for index, panel, value in zip(slots, panels, mine):
        theirs = panel.astype(jnp.float32) * (1.0 / SCALE)
        out = put(out, jnp.where(middle, value, theirs), index)
    return out.reshape(ncolumns * block, ngroups, block)


def plain(descriptors):
    squares = jnp.sum(descriptors * descriptors, axis=1, keepdims=True)
    unit = (descriptors * lax.rsqrt(squares + 1e-06)).astype(jnp.bfloat16)
    columns = lax.all_gather(unit, "grp", axis=0, tiled=True)
    rows = lax.all_gather(unit, "col", axis=0, tiled=True)
    intersection = jnp.dot(rows, columns.T, preferred_element_type=jnp.float32)
    second = intersection * intersection
    return (second * second).reshape(rows.shape[0], -1, unit.shape[0])


def solution(mesh):
    ngroups, ncolumns = mesh.shape["grp"], mesh.shape["col"]
    fits = ncolumns % (2 * LINE) == 0 and ngroups % 2 == 0
    return jax.shard_map(
        shards if fits else plain,
        mesh=mesh,
        in_specs=(P(AXES, None),),
        out_specs=P("grp", None, "col"),
        check_vma=False,
    )
```

```python
import functools

import jax
import jax.numpy as jnp
from jax import lax
from jax.experimental import pallas as pl
from jax.experimental.pallas import tpu as pltpu
from jax.sharding import PartitionSpec as P


AXES = ("grp", "col")
LINE = 4
SCALE = 32768.0


VMEM = pl.BlockSpec(memory_space=pltpu.VMEM)


def unit_kernel(cut, data, first, second):
    squares = jnp.sum(data[...] * data[...], axis=0, keepdims=True)
    scale = lax.rsqrt(squares + 1e-06)
    first[...] = (data[:cut] * scale).astype(jnp.bfloat16)
    second[...] = (data[cut:] * scale).astype(jnp.bfloat16)


def normalize(data, cut):
    features, block = data.shape
    return pl.pallas_call(
        functools.partial(unit_kernel, cut),
        out_shape=[
            jax.ShapeDtypeStruct((cut, block), jnp.bfloat16),
            jax.ShapeDtypeStruct((features - cut, block), jnp.bfloat16),
        ],
        in_specs=[VMEM],
        out_specs=[VMEM, VMEM],
        cost_estimate=pl.CostEstimate(flops=0, bytes_accessed=6 * data.size, transcendentals=0),
        compiler_params=pltpu.CompilerParams(vmem_limit_bytes=8 * data.size),
        name="normalize",
    )(data)


def store_kernel(count, slots, *refs):
    panels, out, sems = refs[:count], refs[count], refs[count + 1]

    def copy(i):
        return pltpu.make_async_copy(panels[i], out.at[slots[i]], sems.at[i])

    for i in range(count):
        copy(i).start()
    for i in range(count):
        copy(i).wait()


def store(panels, slots, length):
    count, shape = len(panels), panels[0].shape
    size = count * panels[0].size
    return pl.pallas_call(
        functools.partial(store_kernel, count),
        out_shape=jax.ShapeDtypeStruct((length,) + shape, panels[0].dtype),
        in_specs=[pl.BlockSpec(memory_space=pltpu.SMEM)]
        + [pl.BlockSpec(memory_space=pl.ANY)] * count,
        out_specs=pl.BlockSpec(memory_space=pltpu.HBM),
        scratch_shapes=[pltpu.SemaphoreType.DMA((count,))],
        cost_estimate=pl.CostEstimate(flops=0, bytes_accessed=8 * size, transcendentals=0),
        compiler_params=pltpu.CompilerParams(vmem_limit_bytes=2**20),
        name="store",
    )(slots, *panels)


def shards(descriptors):
    return exchange(descriptors)


def exchange(descriptors):
    ngroups = lax.axis_size("grp")
    ncolumns = lax.axis_size("col")
    block = descriptors.shape[0]
    inner = ncolumns // LINE
    offsets = range(1, inner)
    others = range(2, ngroups, 2)
    halves = (0, 1)
    grp = lax.axis_index("grp")
    col = lax.axis_index("col")
    z, x = col // inner, col % inner
    middle = jnp.logical_or(z == 1, z == 2)

    def slot(dz, k):
        return (z ^ dz) * inner + (x + k) % inner

    def where(for_middle, for_end):
        return jnp.where(middle, slot(*for_middle), slot(*for_end))

    indices = {("own", j): (grp + j) % ngroups for j in range(0, ngroups, 2)}
    indices.update({("swapped", j): ((grp ^ 1) + j) % ngroups for j in range(0, ngroups, 2)})
    indices.update({"unit": slot(0, 0), "pair": slot(1, 0), "head": where((3, 0), (0, 1))})
    indices.update({"head_pair": where((1, 1), (2, 0)), "relay": where((2, 0), (1, inner - 1))})
    indices.update({("across", k): where((0, k), (0, k + 1)) for k in range(1, inner - 1)})
    indices.update({("across_pair", k): where((1, k), (1, k - 1)) for k in range(2, inner)})
    indices["back", 0] = where((0, inner - 1), (3, 0))
    indices.update({("back", k): where((3, k), (2, k)) for k in offsets})
    indices.update({("far", k): where((2, k), (3, k)) for k in offsets})
    names = list(indices)
    data = descriptors.T
    cut = data.shape[0] // 32 * 16
    unit = normalize(data, cut)
    stored = ["unit", "pair", "head"] + [("across", k) for k in range(1, inner - 1)]
    stored += ["head_pair", "relay"] + [("across_pair", k) for k in range(2, inner)]
    stored += [("back", k) for k in range(inner)]
    slots = jnp.stack([indices[n] for n in stored])
    held = lax.optimization_barrier((*unit, middle, slots, *(indices[n] for n in names)))
    unit, middle, slots = list(held[:2]), held[2], held[3]
    at = dict(zip(names, held[4:]))

    def mid(zz):
        return zz in (1, 2)

    def send(array, move):
        pairs = []
        for g in range(ngroups):
            for c in range(ncolumns):
                tg, tz, tx = move(g, c // inner, c % inner)
                pairs.append((g * ncolumns + c, (tg * LINE + tz) * inner + tx % inner))
        return lax.ppermute(array, AXES, pairs)

    def line_swap(g, zz, xx):
        return g, zz ^ 1, xx

    def centre_swap(k):
        if k % inner == 0:
            return lambda g, zz, xx: (g, zz ^ 3, xx) if mid(zz) else (g ^ 1, zz, xx)
        return lambda g, zz, xx: (g, zz ^ 3, xx) if mid(zz) else (g, zz, xx - k)

    def shift(k, ends):
        if ends % inner == 0:
            return lambda g, zz, xx: (g, zz, xx - k) if mid(zz) else (g ^ 1, zz, xx)
        return lambda g, zz, xx: (g, zz, xx - (k if mid(zz) else ends))

    def other(j):
        return lambda g, zz, xx: ((g - j) % ngroups, zz, xx)

    def core_swap(g, zz, xx):
        return g ^ 1, zz, xx

    def other_core(j):
        return lambda g, zz, xx: (((g ^ 1) - j) % ngroups, zz, xx)

    head, pair, relay, head_pair = ([None, None] for _ in range(4))
    across, centre_across = ([[None, None] for _ in offsets] for _ in range(2))
    across_pair = [[None, None] for _ in range(2, inner)]
    quarter = unit[1].shape[0] // 32 * 16
    own = {0: [(0, unit[0]), (cut, unit[1])]}
    end = {0: []}
    for j in others:
        own[j], end[j] = [], []
    for h in halves:
        head[h] = send(unit[h], centre_swap(1))
        pair[h] = send(unit[h], line_swap)
        for k in offsets:
            across[k - 1][h] = send(unit[h], shift(k, k + 1))
        for j in others:
            own[j].append((h * cut, send(unit[h] if h == 0 else unit[1][:quarter], other(j))))
    swapped = {("own", 0, h): send(unit[h], core_swap) for h in halves}
    for h in halves:
        end[0].append((h * cut, pair[h]))
        for j in others:
            end[j].append((h * cut, send(pair[h], other(j))))
        relay[h] = send(pair[h], centre_swap(inner - 1))
        for k in offsets:
            centre_across[k - 1][h] = send(head[h], shift(k, 0))
        head_pair[h] = send(head[h], line_swap)
        for k in range(2, inner):
            across_pair[k - 2][h] = send(across[k - 2][h], line_swap)
    for j in others:
        own[j].append((cut + quarter, send(unit[1][quarter:], other(j))))
        swapped["own", j, 2] = send(unit[1][quarter:], other_core(j))

    def swap_cores(name, parts, j, i):
        swapped[name, j, i] = send(parts[j][i][1], core_swap)

    for j in others:
        swap_cores("own", own, j, 0)
        swap_cores("own", own, j, 1)
    swap_cores("end", end, 0, 0)
    swap_cores("end", end, 0, 1)
    for j in others:
        swap_cores("end", end, j, 0)
    far_across = [[None, None] for _ in offsets]
    for k in offsets:
        source = head_pair if k == 1 else across_pair[k - 2]
        far_across[k - 1][0] = send(source[0], centre_swap(0))
    for j in others:
        swap_cores("end", end, j, 1)
    for k in offsets:
        far_across[k - 1][1] = send(relay[1], shift(k, 0))

    def place(full, name, parts, last):
        for j in sorted(parts):
            for i, (row, part) in enumerate(parts[j]):
                if (name == "own" and i == 2) != last:
                    continue
                pieces = ((part, at["own", j]), (swapped[name, j, i], at["swapped", j]))
                for array, index in pieces:
                    full = lax.dynamic_update_slice(
                        full, array[None], (index, row, 0), allow_negative_indices=False
                    )
        return full

    def fourth(block, cols):
        intersection = lax.dot_general(
            jnp.concatenate(block, axis=0),
            cols,
            (((0,), (1,)), ((), ())),
            preferred_element_type=jnp.float32,
        )
        second = intersection * intersection
        return second * second

    def product(block):
        return lax.optimization_barrier(fourth(block, columns))

    def put(out, value, index):
        return lax.dynamic_update_index_in_dim(
            out, value, index, 0, allow_negative_indices=False
        )

    def back(block):
        panel = (fourth(block, end_columns) * SCALE).astype(jnp.float16)
        return send(panel, line_swap)

    empty = jnp.zeros((ngroups,) + data.shape, jnp.bfloat16)
    columns = place(empty, "own", own, False)
    end_columns = place(empty, "end", end, False)
    panels = [back(b) for b in [relay] + centre_across]
    columns = place(columns, "own", own, True)
    ready = [(product(unit), "unit"), (product(pair), "pair"), (product(head), "head")]
    ready += [(product(across[k - 1]), ("across", k)) for k in range(1, inner - 1)]
    mine = [product(across[-1])]
    ready += [(product(relay), "relay")]
    panels += [back(b) for b in far_across]
    ready += [(product(head_pair), "head_pair")]
    ready += [(product(across_pair[k - 2]), ("across_pair", k)) for k in range(2, inner)]
    mine += [product(b) for b in centre_across]
    mine += [product(b) for b in far_across]
    merged = [
        jnp.where(middle, value, panel.astype(jnp.float32) * (1.0 / SCALE))
        for value, panel in zip(mine, panels)
    ]
    ready += [(value, ("back", k)) for k, value in enumerate(merged[:inner])]
    ready.sort(key=lambda item: stored.index(item[1]))
    out = store([value for value, _ in ready], slots, ncolumns)
    for k in offsets:
        out = put(out, merged[inner + k - 1], at["far", k])
    return out.reshape(ncolumns * block, ngroups, block)


def plain(descriptors):
    squares = jnp.sum(descriptors * descriptors, axis=1, keepdims=True)
    unit = (descriptors * lax.rsqrt(squares + 1e-06)).astype(jnp.bfloat16)
    columns = lax.all_gather(unit, "grp", axis=0, tiled=True)
    rows = lax.all_gather(unit, "col", axis=0, tiled=True)
    intersection = jnp.dot(rows, columns.T, preferred_element_type=jnp.float32)
    second = intersection * intersection
    return (second * second).reshape(rows.shape[0], -1, unit.shape[0])


def solution(mesh):
    ngroups, ncolumns = mesh.shape["grp"], mesh.shape["col"]
    fits = ncolumns % (2 * LINE) == 0 and ngroups % 2 == 0
    return jax.shard_map(
        shards if fits else plain,
        mesh=mesh,
        in_specs=(P(AXES, None),),
        out_specs=P("grp", None, "col"),
        check_vma=False,
    )
```

```python
import functools
import jax
import jax.numpy as jnp
from jax import lax
from jax.experimental import pallas as pl
from jax.experimental.pallas import tpu as pltpu
from jax.sharding import PartitionSpec as P


AXES = ("grp", "col")
LINE = 4
SCALE = 32768.0
ORDER = (
    "head0", "pair0", "across0", "own0", "head1", "pair1", "across1", "own1",
    "unitcore0", "unitcore1",
    "relay0", "end0", "turn0", "headpair0", "relay1", "end1", "turn1", "headpair1",
    "own2", "crossed0", "owncore0", "owncore1", "paircore0", "paircore1", "endcore0",
    "early*", "far0", "endcore1", "far1", "ends*", "relay>", "turn>",
    "rest*", "unit*", "pair*", "head*", "across*", "relay*", "far>",
    "headpair*", "turn*", "far*",
)


VMEM = pl.BlockSpec(memory_space=pltpu.VMEM)


def unit_kernel(cut, data, first, second):
    squares = jnp.sum(data[...] * data[...], axis=0, keepdims=True)
    scale = lax.rsqrt(squares + 1e-06)
    first[...] = (data[:cut] * scale).astype(jnp.bfloat16)
    second[...] = (data[cut:] * scale).astype(jnp.bfloat16)


def normalize(data, cut):
    features, block = data.shape
    return pl.pallas_call(
        functools.partial(unit_kernel, cut),
        out_shape=[
            jax.ShapeDtypeStruct((cut, block), jnp.bfloat16),
            jax.ShapeDtypeStruct((features - cut, block), jnp.bfloat16),
        ],
        in_specs=[VMEM],
        out_specs=[VMEM, VMEM],
        cost_estimate=pl.CostEstimate(flops=0, bytes_accessed=6 * data.size, transcendentals=0),
        compiler_params=pltpu.CompilerParams(vmem_limit_bytes=8 * data.size),
        name="normalize",
    )(data)


def store_kernel(count, slots, *refs):
    panels, out, sems = refs[:count], refs[count], refs[count + 1]

    def copy(i, a):
        return pltpu.make_async_copy(
            panels[i].at[a], out.at[slots[i], :, a, :], sems.at[i, a]
        )

    pairs = [(i, a) for i in range(count) for a in range(out.shape[2])]
    for pair in pairs:
        copy(*pair).start()
    for pair in pairs:
        copy(*pair).wait()


def store(panels, slots, length):
    count, (rows, nparts, size) = len(panels), panels[0].shape
    total = count * panels[0].size
    return pl.pallas_call(
        functools.partial(store_kernel, count),
        out_shape=jax.ShapeDtypeStruct((length, rows, nparts, size), panels[0].dtype),
        in_specs=[pl.BlockSpec(memory_space=pltpu.SMEM)]
        + [pl.BlockSpec(memory_space=pl.ANY)] * count,
        out_specs=pl.BlockSpec(memory_space=pltpu.HBM),
        scratch_shapes=[pltpu.SemaphoreType.DMA((count, nparts))],
        cost_estimate=pl.CostEstimate(flops=0, bytes_accessed=8 * total, transcendentals=0),
        compiler_params=pltpu.CompilerParams(vmem_limit_bytes=2**20),
        name="store",
    )(slots, *[panel.transpose(1, 0, 2) for panel in panels])


def shards(descriptors):
    return exchange(descriptors)


def exchange(descriptors):
    ngroups = lax.axis_size("grp")
    ncolumns = lax.axis_size("col")
    block = descriptors.shape[0]
    inner = ncolumns // LINE
    offsets = range(1, inner)
    others = range(2, ngroups, 2)
    halves = (0, 1)
    grp = lax.axis_index("grp")
    col = lax.axis_index("col")
    z, x = col // inner, col % inner
    middle = jnp.logical_or(z == 1, z == 2)

    def slot(dz, k):
        return (z ^ dz) * inner + (x + k) % inner

    def where(for_middle, for_end):
        return jnp.where(middle, slot(*for_middle), slot(*for_end))

    indices = {("own", j): (grp + j) % ngroups for j in range(0, ngroups, 2)}
    indices.update({("swapped", j): ((grp ^ 1) + j) % ngroups for j in range(0, ngroups, 2)})
    indices.update({"unit": slot(0, 0), "pair": slot(1, 0), "head": where((3, 0), (0, 1))})
    indices.update({"head_pair": where((1, 1), (2, 0)), "relay": where((2, 0), (1, inner - 1))})
    indices.update({("across", k): where((0, k), (0, k + 1)) for k in range(1, inner - 1)})
    indices.update({("across_pair", k): where((1, k), (1, k - 1)) for k in range(2, inner)})
    indices["back", 0] = where((0, inner - 1), (3, 0))
    indices.update({("back", k): where((3, k), (2, k)) for k in offsets})
    indices.update({("far", k): where((2, k), (3, k)) for k in offsets})
    names = list(indices)
    data = descriptors.T
    cut = data.shape[0] // 32 * 16
    unit = normalize(data, cut)
    stored = ["unit", "pair", "head"] + [("across", k) for k in range(1, inner - 1)]
    stored += ["head_pair", "relay"] + [("across_pair", k) for k in range(2, inner)]
    stored += [("back", k) for k in range(inner)]
    slots = jnp.stack([indices[n] for n in stored])
    held = lax.optimization_barrier((*unit, middle, slots, *(indices[n] for n in names)))
    unit, middle, slots = list(held[:2]), held[2], held[3]
    at = dict(zip(names, held[4:]))

    def mid(zz):
        return zz in (1, 2)

    def send(array, move):
        pairs = []
        for g in range(ngroups):
            for c in range(ncolumns):
                tg, tz, tx = move(g, c // inner, c % inner)
                pairs.append((g * ncolumns + c, (tg * LINE + tz) * inner + tx % inner))
        return lax.ppermute(array, AXES, pairs)

    def line_swap(g, zz, xx):
        return g, zz ^ 1, xx

    def centre_swap(k):
        if k % inner == 0:
            return lambda g, zz, xx: (g, zz ^ 3, xx) if mid(zz) else (g ^ 1, zz, xx)
        return lambda g, zz, xx: (g, zz ^ 3, xx) if mid(zz) else (g, zz, xx - k)

    def shift(k, ends):
        if ends % inner == 0:
            return lambda g, zz, xx: (g, zz, xx - k) if mid(zz) else (g ^ 1, zz, xx)
        return lambda g, zz, xx: (g, zz, xx - (k if mid(zz) else ends))

    def other(j):
        return lambda g, zz, xx: ((g - j) % ngroups, zz, xx)

    def core_swap(g, zz, xx):
        return g ^ 1, zz, xx

    def other_core(j):
        return lambda g, zz, xx: (((g ^ 1) - j) % ngroups, zz, xx)

    quarter = unit[1].shape[0] // 32 * 16
    head, pair, relay, head_pair = ([None, None] for _ in range(4))
    across, centre_across, far = ([[None, None] for _ in offsets] for _ in range(3))
    across_pair = [[None, None] for _ in range(2, inner)]
    own = {j: [None, None, None] for j in others}
    end = {j: [None, None] for j in others}
    own_swapped = {j: [None, None, None] for j in range(0, ngroups, 2)}
    end_swapped = {j: [None, None] for j in range(0, ngroups, 2)}
    columns = {}
    values = {}
    panels = {}

    def place(full, row, part, swapped, j):
        for array, index in ((part, at["own", j]), (swapped, at["swapped", j])):
            full = lax.dynamic_update_slice(
                full, array[None], (index, row, 0), allow_negative_indices=False
            )
        return full

    def fourth(block, cols):
        intersection = lax.dot_general(
            jnp.concatenate(block, axis=0),
            cols,
            (((0,), (1,)), ((), ())),
            preferred_element_type=jnp.float32,
        )
        second = intersection * intersection
        return second * second

    def product(block):
        return lax.optimization_barrier(fourth(block, columns["own"]))

    def fill_early():
        full = jnp.zeros((ngroups,) + data.shape, jnp.bfloat16)
        for h in halves:
            full = place(full, h * cut, unit[h], own_swapped[0][h], 0)
            for j in others:
                full = place(full, h * cut, own[j][h], own_swapped[j][h], j)
        columns["own"] = full

    def fill_rest():
        for j in others:
            full = columns["own"]
            columns["own"] = place(full, cut + quarter, own[j][2], own_swapped[j][2], j)

    def fill_end():
        full = jnp.zeros((ngroups,) + data.shape, jnp.bfloat16)
        for h in halves:
            full = place(full, h * cut, pair[h], end_swapped[0][h], 0)
            for j in others:
                full = place(full, h * cut, end[j][h], end_swapped[j][h], j)
        columns["end"] = full

    def piece(i):
        return (unit[0], unit[1][:quarter], unit[1][quarter:])[i]

    def run(name):
        what, h = (name[:-1], int(name[-1])) if name[-1].isdigit() else ("", 0)
        if what == "head":
            head[h] = send(unit[h], centre_swap(1))
        elif what == "pair":
            pair[h] = send(unit[h], line_swap)
        elif what == "across":
            for k in offsets:
                across[k - 1][h] = send(unit[h], shift(k, k + 1))
        elif what == "own":
            for j in others:
                own[j][h] = send(piece(h), other(j))
        elif what == "crossed":
            for j in others:
                own_swapped[j][2] = send(piece(2), other_core(j))
        elif what == "unitcore":
            own_swapped[0][h] = send(unit[h], core_swap)
        elif what == "owncore":
            for j in others:
                own_swapped[j][h] = send(own[j][h], core_swap)
        elif what == "paircore":
            end_swapped[0][h] = send(pair[h], core_swap)
        elif what == "endcore":
            for j in others:
                end_swapped[j][h] = send(end[j][h], core_swap)
        elif what == "relay":
            relay[h] = send(pair[h], centre_swap(inner - 1))
        elif what == "turn":
            for k in offsets:
                centre_across[k - 1][h] = send(head[h], shift(k, 0))
        elif what == "headpair":
            head_pair[h] = send(head[h], line_swap)
            for k in range(2, inner):
                across_pair[k - 2][h] = send(across[k - 2][h], line_swap)
        elif what == "end":
            for j in others:
                end[j][h] = send(pair[h], other(j))
        elif what == "far":
            for k in offsets:
                source = head_pair if k == 1 else across_pair[k - 2]
                if h == 0:
                    far[k - 1][0] = send(source[0], centre_swap(0))
                else:
                    far[k - 1][1] = send(relay[1], shift(k, 0))
        elif name == "early*":
            fill_early()
        elif name == "rest*":
            fill_rest()
        elif name == "ends*":
            fill_end()
        elif name == "unit*":
            values["unit"] = product(unit)
        elif name == "pair*":
            values["pair"] = product(pair)
        elif name == "head*":
            values["head"] = product(head)
        elif name == "across*":
            for k in range(1, inner - 1):
                values["across", k] = product(across[k - 1])
            values["back", 0] = product(across[-1])
        elif name == "headpair*":
            values["head_pair"] = product(head_pair)
            for k in range(2, inner):
                values["across_pair", k] = product(across_pair[k - 2])
        elif name == "relay*":
            values["relay"] = product(relay)
        elif name == "turn*":
            for k in offsets:
                values["back", k] = product(centre_across[k - 1])
        elif name == "far*":
            for k in offsets:
                values["far", k] = product(far[k - 1])

    def panel(block):
        return (fourth(block, columns["end"]) * SCALE).astype(jnp.float16)

    sources = {
        "relay>": [(relay, ("back", 0))],
        "turn>": [(b, ("back", k)) for k, b in zip(offsets, centre_across)],
        "far>": [(b, ("far", k)) for k, b in zip(offsets, far)],
    }
    for name in ORDER:
        if name in sources:
            made = [(panel(b), key) for b, key in sources[name]]
            for value, key in made:
                panels[key] = send(value, line_swap)
        else:
            run(name)

    for key, value in panels.items():
        values[key] = jnp.where(middle, values[key], value.astype(jnp.float32) * (1.0 / SCALE))
    out = store([values[key] for key in stored], slots, ncolumns)
    for k in offsets:
        out = lax.dynamic_update_index_in_dim(
            out, values["far", k], at["far", k], 0, allow_negative_indices=False
        )
    return out.reshape(ncolumns * block, ngroups, block)


def plain(descriptors):
    squares = jnp.sum(descriptors * descriptors, axis=1, keepdims=True)
    unit = (descriptors * lax.rsqrt(squares + 1e-06)).astype(jnp.bfloat16)
    columns = lax.all_gather(unit, "grp", axis=0, tiled=True)
    rows = lax.all_gather(unit, "col", axis=0, tiled=True)
    intersection = jnp.dot(rows, columns.T, preferred_element_type=jnp.float32)
    second = intersection * intersection
    return (second * second).reshape(rows.shape[0], -1, unit.shape[0])


def solution(mesh):
    ngroups, ncolumns = mesh.shape["grp"], mesh.shape["col"]
    fits = ncolumns % (2 * LINE) == 0 and ngroups % 2 == 0
    return jax.shard_map(
        shards if fits else plain,
        mesh=mesh,
        in_specs=(P(AXES, None),),
        out_specs=P("grp", None, "col"),
        check_vma=False,
    )
```

```python
import functools
import jax
import jax.numpy as jnp
from jax import lax
from jax.experimental import pallas as pl
from jax.experimental.pallas import tpu as pltpu
from jax.sharding import PartitionSpec as P


AXES = ("grp", "col")
LINE = 4
SCALE = 32768.0
ORDER = (
    "head0", "pair0", "across0", "own0", "head1", "pair1", "across1", "own1",
    "unitcore0", "unitcore1", "relay0", "end0", "turn0", "headpair0", "relay1", "end1",
    "turn1", "headpair1", "own2", "crossed0", "owncore0", "owncore1", "paircore0", "paircore1",
    "endcore0", "early*", "far0", "far1", "endcore1", "ends*", "relay>", "turn>",
    "rest*", "unit*", "pair*", "head*", "across*", "relay*", "far>", "headpair*",
    "turn*", "far*",
)


VMEM = pl.BlockSpec(memory_space=pltpu.VMEM)


def unit_kernel(cut, chunks, source, first, second, data, sems):
    size = data.shape[0] // chunks

    def load(i):
        span = pl.ds(i * size, size)
        return pltpu.make_async_copy(source.at[span], data.at[span], sems.at[i])

    for i in range(chunks):
        load(i).start()
    squares = jnp.zeros((1, data.shape[1]), jnp.float32)
    for i in range(chunks):
        load(i).wait()
        part = data[i * size : (i + 1) * size]
        squares += jnp.sum(part * part, axis=0, keepdims=True)
    scale = lax.rsqrt(squares + 1e-06)
    first[...] = (data[:cut] * scale).astype(jnp.bfloat16)
    second[...] = (data[cut:] * scale).astype(jnp.bfloat16)


def normalize(data, cut):
    features, block = data.shape
    chunks = next(n for n in (5, 4, 3, 2, 1) if features % (8 * n) == 0)
    return pl.pallas_call(
        functools.partial(unit_kernel, cut, chunks),
        out_shape=[
            jax.ShapeDtypeStruct((cut, block), jnp.bfloat16),
            jax.ShapeDtypeStruct((features - cut, block), jnp.bfloat16),
        ],
        in_specs=[pl.BlockSpec(memory_space=pltpu.HBM)],
        out_specs=[VMEM, VMEM],
        scratch_shapes=[
            pltpu.VMEM((features, block), jnp.float32),
            pltpu.SemaphoreType.DMA((chunks,)),
        ],
        cost_estimate=pl.CostEstimate(flops=0, bytes_accessed=6 * data.size, transcendentals=0),
        compiler_params=pltpu.CompilerParams(vmem_limit_bytes=16 * data.size),
        name="normalize",
    )(pltpu.with_memory_space_constraint(data, pltpu.HBM))


def store_kernel(count, slots, *refs):
    panels, out, sems = refs[:count], refs[count], refs[count + 1]

    def copy(i, a):
        return pltpu.make_async_copy(
            panels[i].at[a], out.at[slots[i], :, a, :], sems.at[i, a]
        )

    pairs = [(i, a) for i in range(count) for a in range(out.shape[2])]
    for pair in pairs:
        copy(*pair).start()
    for pair in pairs:
        copy(*pair).wait()


def store(panels, slots, length):
    count, (rows, nparts, size) = len(panels), panels[0].shape
    total = count * panels[0].size
    return pl.pallas_call(
        functools.partial(store_kernel, count),
        out_shape=jax.ShapeDtypeStruct((length, rows, nparts, size), panels[0].dtype),
        in_specs=[pl.BlockSpec(memory_space=pltpu.SMEM)]
        + [pl.BlockSpec(memory_space=pl.ANY)] * count,
        out_specs=pl.BlockSpec(memory_space=pltpu.HBM),
        scratch_shapes=[pltpu.SemaphoreType.DMA((count, nparts))],
        cost_estimate=pl.CostEstimate(flops=0, bytes_accessed=8 * total, transcendentals=0),
        compiler_params=pltpu.CompilerParams(vmem_limit_bytes=2**20),
        name="store",
    )(slots, *[panel.transpose(1, 0, 2) for panel in panels])


def blank_kernel(*refs):
    del refs


def blank(after, shape, count):
    return pl.pallas_call(
        blank_kernel,
        out_shape=[jax.ShapeDtypeStruct(shape, jnp.bfloat16)] * count,
        in_specs=[pl.BlockSpec(memory_space=pl.ANY)],
        out_specs=[pl.BlockSpec(memory_space=pl.ANY)] * count,
        cost_estimate=pl.CostEstimate(flops=0, bytes_accessed=0, transcendentals=0),
        compiler_params=pltpu.CompilerParams(vmem_limit_bytes=2**20),
        name="blank",
    )(after)


def shards(descriptors):
    return exchange(descriptors)


def exchange(descriptors):
    ngroups = lax.axis_size("grp")
    ncolumns = lax.axis_size("col")
    block = descriptors.shape[0]
    inner = ncolumns // LINE
    offsets = range(1, inner)
    others = range(2, ngroups, 2)
    halves = (0, 1)
    grp = lax.axis_index("grp")
    col = lax.axis_index("col")
    z, x = col // inner, col % inner
    middle = jnp.logical_or(z == 1, z == 2)

    def slot(dz, k):
        return (z ^ dz) * inner + (x + k) % inner

    def where(for_middle, for_end):
        return jnp.where(middle, slot(*for_middle), slot(*for_end))

    indices = {("own", j): (grp + j) % ngroups for j in range(0, ngroups, 2)}
    indices.update({("swapped", j): ((grp ^ 1) + j) % ngroups for j in range(0, ngroups, 2)})
    indices.update({"unit": slot(0, 0), "pair": slot(1, 0), "head": where((3, 0), (0, 1))})
    indices.update({"head_pair": where((1, 1), (2, 0)), "relay": where((2, 0), (1, inner - 1))})
    indices.update({("across", k): where((0, k), (0, k + 1)) for k in range(1, inner - 1)})
    indices.update({("across_pair", k): where((1, k), (1, k - 1)) for k in range(2, inner)})
    indices["back", 0] = where((0, inner - 1), (3, 0))
    indices.update({("back", k): where((3, k), (2, k)) for k in offsets})
    indices.update({("far", k): where((2, k), (3, k)) for k in offsets})
    names = list(indices)
    data = descriptors.T
    cut = data.shape[0] // 32 * 16
    unit = normalize(data, cut)
    stored = ["unit", "pair", "head"] + [("across", k) for k in range(1, inner - 1)]
    stored += ["head_pair", "relay"] + [("across_pair", k) for k in range(2, inner)]
    stored += [("back", k) for k in range(inner)]
    slots = jnp.stack([indices[n] for n in stored])
    held = lax.optimization_barrier((*unit, middle, slots, *(indices[n] for n in names)))
    unit, middle, slots = list(held[:2]), held[2], held[3]
    at = dict(zip(names, held[4:]))

    def mid(zz):
        return zz in (1, 2)

    def send(array, move):
        pairs = []
        for g in range(ngroups):
            for c in range(ncolumns):
                tg, tz, tx = move(g, c // inner, c % inner)
                pairs.append((g * ncolumns + c, (tg * LINE + tz) * inner + tx % inner))
        return lax.ppermute(array, AXES, pairs)

    def line_swap(g, zz, xx):
        return g, zz ^ 1, xx

    def centre_swap(k):
        if k % inner == 0:
            return lambda g, zz, xx: (g, zz ^ 3, xx) if mid(zz) else (g ^ 1, zz, xx)
        return lambda g, zz, xx: (g, zz ^ 3, xx) if mid(zz) else (g, zz, xx - k)

    def shift(k, ends):
        if ends % inner == 0:
            return lambda g, zz, xx: (g, zz, xx - k) if mid(zz) else (g ^ 1, zz, xx)
        return lambda g, zz, xx: (g, zz, xx - (k if mid(zz) else ends))

    def other(j):
        return lambda g, zz, xx: ((g - j) % ngroups, zz, xx)

    def core_swap(g, zz, xx):
        return g ^ 1, zz, xx

    def other_core(j):
        return lambda g, zz, xx: (((g ^ 1) - j) % ngroups, zz, xx)

    quarter = unit[1].shape[0] // 32 * 16
    head, pair, relay, head_pair = ([None, None] for _ in range(4))
    across, centre_across, far = ([[None, None] for _ in offsets] for _ in range(3))
    across_pair = [[None, None] for _ in range(2, inner)]
    own = {j: [None, None, None] for j in others}
    end = {j: [None, None] for j in others}
    own_swapped = {j: [None, None, None] for j in range(0, ngroups, 2)}
    end_swapped = {j: [None, None] for j in range(0, ngroups, 2)}
    blanks = list(blank(unit[0], (ngroups,) + data.shape, 2))
    columns = {}
    values = {}
    panels = {}

    def place(full, row, part, swapped, j):
        for array, index in ((part, at["own", j]), (swapped, at["swapped", j])):
            full = lax.dynamic_update_slice(
                full, array[None], (index, row, 0), allow_negative_indices=False
            )
        return full

    def fourth(block, cols):
        intersection = lax.dot_general(
            jnp.concatenate(block, axis=0),
            cols,
            (((0,), (1,)), ((), ())),
            preferred_element_type=jnp.float32,
        )
        second = intersection * intersection
        return second * second

    def product(block):
        return lax.optimization_barrier(fourth(block, columns["own"]))

    def fill_early():
        full = blanks.pop()
        for h in halves:
            full = place(full, h * cut, unit[h], own_swapped[0][h], 0)
            for j in others:
                full = place(full, h * cut, own[j][h], own_swapped[j][h], j)
        columns["own"] = full

    def fill_rest():
        for j in others:
            full = columns["own"]
            columns["own"] = place(full, cut + quarter, own[j][2], own_swapped[j][2], j)

    def fill_end():
        full = blanks.pop()
        for h in halves:
            full = place(full, h * cut, pair[h], end_swapped[0][h], 0)
            for j in others:
                full = place(full, h * cut, end[j][h], end_swapped[j][h], j)
        columns["end"] = full

    def piece(i):
        return (unit[0], unit[1][:quarter], unit[1][quarter:])[i]

    def run(name):
        what, h = (name[:-1], int(name[-1])) if name[-1].isdigit() else ("", 0)
        if what == "head":
            head[h] = send(unit[h], centre_swap(1))
        elif what == "pair":
            pair[h] = send(unit[h], line_swap)
        elif what == "across":
            for k in offsets:
                across[k - 1][h] = send(unit[h], shift(k, k + 1))
        elif what == "own":
            for j in others:
                own[j][h] = send(piece(h), other(j))
        elif what == "crossed":
            for j in others:
                own_swapped[j][2] = send(piece(2), other_core(j))
        elif what == "unitcore":
            own_swapped[0][h] = send(unit[h], core_swap)
        elif what == "owncore":
            for j in others:
                own_swapped[j][h] = send(own[j][h], core_swap)
        elif what == "paircore":
            end_swapped[0][h] = send(pair[h], core_swap)
        elif what == "endcore":
            for j in others:
                end_swapped[j][h] = send(end[j][h], core_swap)
        elif what == "relay":
            relay[h] = send(pair[h], centre_swap(inner - 1))
        elif what == "turn":
            for k in offsets:
                centre_across[k - 1][h] = send(head[h], shift(k, 0))
        elif what == "headpair":
            head_pair[h] = send(head[h], line_swap)
            for k in range(2, inner):
                across_pair[k - 2][h] = send(across[k - 2][h], line_swap)
        elif what == "end":
            for j in others:
                end[j][h] = send(pair[h], other(j))
        elif what == "far":
            for k in offsets:
                source = head_pair if k == 1 else across_pair[k - 2]
                if h == 0:
                    far[k - 1][0] = send(source[0], centre_swap(0))
                else:
                    far[k - 1][1] = send(relay[1], shift(k, 0))
        elif name == "early*":
            fill_early()
        elif name == "rest*":
            fill_rest()
        elif name == "ends*":
            fill_end()
        elif name == "unit*":
            values["unit"] = product(unit)
        elif name == "pair*":
            values["pair"] = product(pair)
        elif name == "head*":
            values["head"] = product(head)
        elif name == "across*":
            for k in range(1, inner - 1):
                values["across", k] = product(across[k - 1])
            values["back", 0] = product(across[-1])
        elif name == "headpair*":
            values["head_pair"] = product(head_pair)
            for k in range(2, inner):
                values["across_pair", k] = product(across_pair[k - 2])
        elif name == "relay*":
            values["relay"] = product(relay)
        elif name == "turn*":
            for k in offsets:
                values["back", k] = product(centre_across[k - 1])
        elif name == "far*":
            for k in offsets:
                values["far", k] = product(far[k - 1])

    def panel(block):
        return (fourth(block, columns["end"]) * SCALE).astype(jnp.float16)

    sources = {
        "relay>": [(relay, ("back", 0))],
        "turn>": [(b, ("back", k)) for k, b in zip(offsets, centre_across)],
        "far>": [(b, ("far", k)) for k, b in zip(offsets, far)],
    }
    for name in ORDER:
        if name in sources:
            made = [(panel(b), key) for b, key in sources[name]]
            for value, key in made:
                panels[key] = send(value, line_swap)
        else:
            run(name)

    for key, value in panels.items():
        values[key] = jnp.where(middle, values[key], value.astype(jnp.float32) * (1.0 / SCALE))
    out = store([values[key] for key in stored], slots, ncolumns)
    for k in offsets:
        out = lax.dynamic_update_index_in_dim(
            out, values["far", k], at["far", k], 0, allow_negative_indices=False
        )
    return out.reshape(ncolumns * block, ngroups, block)


def plain(descriptors):
    squares = jnp.sum(descriptors * descriptors, axis=1, keepdims=True)
    unit = (descriptors * lax.rsqrt(squares + 1e-06)).astype(jnp.bfloat16)
    columns = lax.all_gather(unit, "grp", axis=0, tiled=True)
    rows = lax.all_gather(unit, "col", axis=0, tiled=True)
    intersection = jnp.dot(rows, columns.T, preferred_element_type=jnp.float32)
    second = intersection * intersection
    return (second * second).reshape(rows.shape[0], -1, unit.shape[0])


def solution(mesh):
    ngroups, ncolumns = mesh.shape["grp"], mesh.shape["col"]
    fits = ncolumns % (2 * LINE) == 0 and ngroups % 2 == 0
    return jax.shard_map(
        shards if fits else plain,
        mesh=mesh,
        in_specs=(P(AXES, None),),
        out_specs=P("grp", None, "col"),
        check_vma=False,
    )
```

```python
import functools
import jax
import jax.numpy as jnp
from jax import lax
from jax.experimental import pallas as pl
from jax.experimental.pallas import tpu as pltpu
from jax.sharding import PartitionSpec as P


AXES = ("grp", "col")
LINE = 4
SCALE = 32768.0
ORDER = (
    "head0", "pair0", "across0", "own0", "head1", "pair1", "across1", "own1",
    "unitcore0", "unitcore1", "relay0", "end0", "turn0", "headpair0", "relay1", "end1",
    "turn1", "headpair1", "own2", "crossed0", "owncore0", "owncore1", "paircore0", "paircore1",
    "endcore0", "early*", "far0", "far1", "endcore1", "ends*", "relay>", "turn>",
    "rest*", "unit*", "pair*", "head*", "across*", "relay*", "far>", "headpair*",
    "turn*", "far*",
)


VMEM = pl.BlockSpec(memory_space=pltpu.VMEM)


def unit_kernel(cut, chunks, source, first, second, data, sems):
    size = data.shape[0] // chunks

    def load(i):
        span = pl.ds(i * size, size)
        return pltpu.make_async_copy(source.at[span], data.at[span], sems.at[i])

    for i in range(chunks):
        load(i).start()
    squares = jnp.zeros((1, data.shape[1]), jnp.float32)
    for i in range(chunks):
        load(i).wait()
        part = data[i * size : (i + 1) * size]
        squares += jnp.sum(part * part, axis=0, keepdims=True)
    scale = lax.rsqrt(squares + 1e-06)
    first[...] = (data[:cut] * scale).astype(jnp.bfloat16)
    second[...] = (data[cut:] * scale).astype(jnp.bfloat16)


def normalize(data, cut):
    features, block = data.shape
    chunks = next(n for n in (10, 5, 2, 1) if features % (8 * n) == 0)
    return pl.pallas_call(
        functools.partial(unit_kernel, cut, chunks),
        out_shape=[
            jax.ShapeDtypeStruct((cut, block), jnp.bfloat16),
            jax.ShapeDtypeStruct((features - cut, block), jnp.bfloat16),
        ],
        in_specs=[pl.BlockSpec(memory_space=pltpu.HBM)],
        out_specs=[VMEM, VMEM],
        scratch_shapes=[
            pltpu.VMEM((features, block), jnp.float32),
            pltpu.SemaphoreType.DMA((chunks,)),
        ],
        cost_estimate=pl.CostEstimate(flops=0, bytes_accessed=6 * data.size, transcendentals=0),
        compiler_params=pltpu.CompilerParams(vmem_limit_bytes=16 * data.size),
        name="normalize",
    )(pltpu.with_memory_space_constraint(data, pltpu.HBM))


def store_kernel(count, slots, *refs):
    panels, out, sems = refs[:count], refs[count], refs[count + 1]

    def copy(i, a):
        return pltpu.make_async_copy(
            panels[i].at[a], out.at[slots[i], :, a, :], sems.at[i, a]
        )

    pairs = [(i, a) for i in range(count) for a in range(out.shape[2])]
    for pair in pairs:
        copy(*pair).start()
    for pair in pairs:
        copy(*pair).wait()


def store(panels, slots, length):
    count, (rows, nparts, size) = len(panels), panels[0].shape
    total = count * panels[0].size
    return pl.pallas_call(
        functools.partial(store_kernel, count),
        out_shape=jax.ShapeDtypeStruct((length, rows, nparts, size), panels[0].dtype),
        in_specs=[pl.BlockSpec(memory_space=pltpu.SMEM)]
        + [pl.BlockSpec(memory_space=pl.ANY)] * count,
        out_specs=pl.BlockSpec(memory_space=pltpu.HBM),
        scratch_shapes=[pltpu.SemaphoreType.DMA((count, nparts))],
        cost_estimate=pl.CostEstimate(flops=0, bytes_accessed=8 * total, transcendentals=0),
        compiler_params=pltpu.CompilerParams(vmem_limit_bytes=2**20),
        name="store",
    )(slots, *[panel.transpose(1, 0, 2) for panel in panels])


def blank_kernel(*refs):
    del refs


def blank(after, shape, count):
    return pl.pallas_call(
        blank_kernel,
        out_shape=[jax.ShapeDtypeStruct(shape, jnp.bfloat16)] * count,
        in_specs=[pl.BlockSpec(memory_space=pl.ANY)],
        out_specs=[pl.BlockSpec(memory_space=pl.ANY)] * count,
        cost_estimate=pl.CostEstimate(flops=0, bytes_accessed=0, transcendentals=0),
        compiler_params=pltpu.CompilerParams(vmem_limit_bytes=2**20),
        name="blank",
    )(after)


def last_kernel(count, slots, *refs):
    panels, out, sems = refs[:count], refs[count + 1], refs[count + 2]

    def copy(i, a):
        return pltpu.make_async_copy(panels[i].at[a], out.at[slots[i], :, a, :], sems.at[i, a])

    pairs = [(i, a) for i in range(count) for a in range(out.shape[2])]
    for pair in pairs:
        copy(*pair).start()
    for pair in pairs:
        copy(*pair).wait()


def store_last(panels, slots, out):
    count = len(panels)
    return pl.pallas_call(
        functools.partial(last_kernel, count),
        out_shape=jax.ShapeDtypeStruct(out.shape, out.dtype),
        in_specs=[pl.BlockSpec(memory_space=pltpu.SMEM)]
        + [pl.BlockSpec(memory_space=pl.ANY)] * count
        + [pl.BlockSpec(memory_space=pltpu.HBM)],
        out_specs=pl.BlockSpec(memory_space=pltpu.HBM),
        input_output_aliases={count + 1: 0},
        scratch_shapes=[pltpu.SemaphoreType.DMA((count, out.shape[2]))],
        cost_estimate=pl.CostEstimate(flops=0, bytes_accessed=2**20, transcendentals=0),
        compiler_params=pltpu.CompilerParams(vmem_limit_bytes=2**20),
        name="store_last",
    )(slots, *[panel.transpose(1, 0, 2) for panel in panels], out)


def shards(descriptors):
    return exchange(descriptors)


def exchange(descriptors):
    ngroups = lax.axis_size("grp")
    ncolumns = lax.axis_size("col")
    block = descriptors.shape[0]
    inner = ncolumns // LINE
    offsets = range(1, inner)
    others = range(2, ngroups, 2)
    halves = (0, 1)
    grp = lax.axis_index("grp")
    col = lax.axis_index("col")
    z, x = col // inner, col % inner
    middle = jnp.logical_or(z == 1, z == 2)

    def slot(dz, k):
        return (z ^ dz) * inner + (x + k) % inner

    def where(for_middle, for_end):
        return jnp.where(middle, slot(*for_middle), slot(*for_end))

    indices = {("own", j): (grp + j) % ngroups for j in range(0, ngroups, 2)}
    indices.update({("swapped", j): ((grp ^ 1) + j) % ngroups for j in range(0, ngroups, 2)})
    indices.update({"unit": slot(0, 0), "pair": slot(1, 0), "head": where((3, 0), (0, 1))})
    indices.update({"head_pair": where((1, 1), (2, 0)), "relay": where((2, 0), (1, inner - 1))})
    indices.update({("across", k): where((0, k), (0, k + 1)) for k in range(1, inner - 1)})
    indices.update({("across_pair", k): where((1, k), (1, k - 1)) for k in range(2, inner)})
    indices["back", 0] = where((0, inner - 1), (3, 0))
    indices.update({("back", k): where((3, k), (2, k)) for k in offsets})
    indices.update({("far", k): where((2, k), (3, k)) for k in offsets})
    names = list(indices)
    data = descriptors.T
    cut = data.shape[0] // 32 * 16
    unit = normalize(data, cut)
    stored = ["unit", "pair", "head"] + [("across", k) for k in range(1, inner - 1)]
    stored += ["head_pair", "relay"] + [("across_pair", k) for k in range(2, inner)]
    stored += [("back", k) for k in range(inner)]
    slots = jnp.stack([indices[n] for n in stored])
    last_slots = jnp.stack([indices["far", k] for k in offsets])
    held = lax.optimization_barrier(
        (*unit, middle, slots, last_slots, *(indices[n] for n in names))
    )
    unit, middle, slots, last_slots = list(held[:2]), held[2], held[3], held[4]
    at = dict(zip(names, held[5:]))

    def mid(zz):
        return zz in (1, 2)

    def send(array, move):
        pairs = []
        for g in range(ngroups):
            for c in range(ncolumns):
                tg, tz, tx = move(g, c // inner, c % inner)
                pairs.append((g * ncolumns + c, (tg * LINE + tz) * inner + tx % inner))
        return lax.ppermute(array, AXES, pairs)

    def line_swap(g, zz, xx):
        return g, zz ^ 1, xx

    def centre_swap(k):
        if k % inner == 0:
            return lambda g, zz, xx: (g, zz ^ 3, xx) if mid(zz) else (g ^ 1, zz, xx)
        return lambda g, zz, xx: (g, zz ^ 3, xx) if mid(zz) else (g, zz, xx - k)

    def shift(k, ends):
        if ends % inner == 0:
            return lambda g, zz, xx: (g, zz, xx - k) if mid(zz) else (g ^ 1, zz, xx)
        return lambda g, zz, xx: (g, zz, xx - (k if mid(zz) else ends))

    def other(j):
        return lambda g, zz, xx: ((g - j) % ngroups, zz, xx)

    def core_swap(g, zz, xx):
        return g ^ 1, zz, xx

    def other_core(j):
        return lambda g, zz, xx: (((g ^ 1) - j) % ngroups, zz, xx)

    quarter = unit[1].shape[0] // 32 * 16
    head, pair, relay, head_pair = ([None, None] for _ in range(4))
    across, centre_across, far = ([[None, None] for _ in offsets] for _ in range(3))
    across_pair = [[None, None] for _ in range(2, inner)]
    own = {j: [None, None, None] for j in others}
    end = {j: [None, None] for j in others}
    own_swapped = {j: [None, None, None] for j in range(0, ngroups, 2)}
    end_swapped = {j: [None, None] for j in range(0, ngroups, 2)}
    blanks = list(blank(unit[0], (ngroups,) + data.shape, 2))
    columns = {}
    values = {}
    panels = {}

    def place(full, row, part, swapped, j):
        for array, index in ((part, at["own", j]), (swapped, at["swapped", j])):
            full = lax.dynamic_update_slice(
                full, array[None], (index, row, 0), allow_negative_indices=False
            )
        return full

    def fourth(block, cols):
        intersection = lax.dot_general(
            jnp.concatenate(block, axis=0),
            cols,
            (((0,), (1,)), ((), ())),
            preferred_element_type=jnp.float32,
        )
        second = intersection * intersection
        return second * second

    def product(block):
        return lax.optimization_barrier(fourth(block, columns["own"]))

    def fill_early():
        full = blanks.pop()
        for h in halves:
            full = place(full, h * cut, unit[h], own_swapped[0][h], 0)
            for j in others:
                full = place(full, h * cut, own[j][h], own_swapped[j][h], j)
        columns["own"] = full

    def fill_rest():
        for j in others:
            full = columns["own"]
            columns["own"] = place(full, cut + quarter, own[j][2], own_swapped[j][2], j)

    def fill_end():
        full = blanks.pop()
        for h in halves:
            full = place(full, h * cut, pair[h], end_swapped[0][h], 0)
            for j in others:
                full = place(full, h * cut, end[j][h], end_swapped[j][h], j)
        columns["end"] = full

    def piece(i):
        return (unit[0], unit[1][:quarter], unit[1][quarter:])[i]

    def run(name):
        what, h = (name[:-1], int(name[-1])) if name[-1].isdigit() else ("", 0)
        if what == "head":
            head[h] = send(unit[h], centre_swap(1))
        elif what == "pair":
            pair[h] = send(unit[h], line_swap)
        elif what == "across":
            for k in offsets:
                across[k - 1][h] = send(unit[h], shift(k, k + 1))
        elif what == "own":
            for j in others:
                own[j][h] = send(piece(h), other(j))
        elif what == "crossed":
            for j in others:
                own_swapped[j][2] = send(piece(2), other_core(j))
        elif what == "unitcore":
            own_swapped[0][h] = send(unit[h], core_swap)
        elif what == "owncore":
            for j in others:
                own_swapped[j][h] = send(own[j][h], core_swap)
        elif what == "paircore":
            end_swapped[0][h] = send(pair[h], core_swap)
        elif what == "endcore":
            for j in others:
                end_swapped[j][h] = send(end[j][h], core_swap)
        elif what == "relay":
            relay[h] = send(pair[h], centre_swap(inner - 1))
        elif what == "turn":
            for k in offsets:
                centre_across[k - 1][h] = send(head[h], shift(k, 0))
        elif what == "headpair":
            head_pair[h] = send(head[h], line_swap)
            for k in range(2, inner):
                across_pair[k - 2][h] = send(across[k - 2][h], line_swap)
        elif what == "end":
            for j in others:
                end[j][h] = send(pair[h], other(j))
        elif what == "far":
            for k in offsets:
                source = head_pair if k == 1 else across_pair[k - 2]
                if h == 0:
                    far[k - 1][0] = send(source[0], centre_swap(0))
                else:
                    far[k - 1][1] = send(relay[1], shift(k, 0))
        elif name == "early*":
            fill_early()
        elif name == "rest*":
            fill_rest()
        elif name == "ends*":
            fill_end()
        elif name == "unit*":
            values["unit"] = product(unit)
        elif name == "pair*":
            values["pair"] = product(pair)
        elif name == "head*":
            values["head"] = product(head)
        elif name == "across*":
            for k in range(1, inner - 1):
                values["across", k] = product(across[k - 1])
            values["back", 0] = product(across[-1])
        elif name == "headpair*":
            values["head_pair"] = product(head_pair)
            for k in range(2, inner):
                values["across_pair", k] = product(across_pair[k - 2])
        elif name == "relay*":
            values["relay"] = product(relay)
        elif name == "turn*":
            for k in offsets:
                values["back", k] = product(centre_across[k - 1])
        elif name == "far*":
            for k in offsets:
                values["far", k] = product(far[k - 1])

    def panel(block):
        return (fourth(block, columns["end"]) * SCALE).astype(jnp.float16)

    sources = {
        "relay>": [(relay, ("back", 0))],
        "turn>": [(b, ("back", k)) for k, b in zip(offsets, centre_across)],
        "far>": [(b, ("far", k)) for k, b in zip(offsets, far)],
    }
    for name in ORDER:
        if name in sources:
            made = [(panel(b), key) for b, key in sources[name]]
            for value, key in made:
                panels[key] = send(value, line_swap)
        else:
            run(name)

    for key, value in panels.items():
        values[key] = jnp.where(middle, values[key], value.astype(jnp.float32) * (1.0 / SCALE))
    out = store([values[key] for key in stored], slots, ncolumns)
    out = store_last([values["far", k] for k in offsets], last_slots, out)
    return out.reshape(ncolumns * block, ngroups, block)


def plain(descriptors):
    squares = jnp.sum(descriptors * descriptors, axis=1, keepdims=True)
    unit = (descriptors * lax.rsqrt(squares + 1e-06)).astype(jnp.bfloat16)
    columns = lax.all_gather(unit, "grp", axis=0, tiled=True)
    rows = lax.all_gather(unit, "col", axis=0, tiled=True)
    intersection = jnp.dot(rows, columns.T, preferred_element_type=jnp.float32)
    second = intersection * intersection
    return (second * second).reshape(rows.shape[0], -1, unit.shape[0])


def solution(mesh):
    ngroups, ncolumns = mesh.shape["grp"], mesh.shape["col"]
    fits = ncolumns % (2 * LINE) == 0 and ngroups % 2 == 0
    return jax.shard_map(
        shards if fits else plain,
        mesh=mesh,
        in_specs=(P(AXES, None),),
        out_specs=P("grp", None, "col"),
        check_vma=False,
    )
```
